32 devices in a mesh: groups: 2 (over x), visit: 8 (over z, y), tile: 2 (over core).
Axes of the slice: x: 2, y: 2, z: 4, core: 2. Of those that a mesh axis runs over, the one named last changes fastest.
Arguments:
- templates: float32 [2, 16, 64, 512], P(None, ('groups', 'visit'), 'tile'), parts along dimension 1, may hold values from -7 to 7
- science: float32 [2, 16, 64, 512], P(None, ('groups', 'visit'), 'tile'), parts along dimension 1, may hold values from -20 to 20
- stamp_mask: int32 [2, 16, 64], P(None, ('groups', 'visit'), 'tile'), parts along dimension 1, may hold values from 0 to 1, as said below
- owner: int32 [4], P('groups'), parts along dimension 0, may hold values from 0 to 7
- visit_map: int32 [16], P('groups'), parts along dimension 0, may hold values from 0 to 7, each once
- vertical: float32 [40, 21], replicated, may hold values from -3 to 3
- horizontal: float32 [40, 21], replicated, may hold values from -3 to 3
- psf: float32 [21, 21], replicated, may hold values from 0 to 0.1
Outputs:
- difference: float32 [2, 16, 64, 512], P(None, ('groups', 'visit'), 'tile'), parts along dimension 1
- likelihood: float32 [2, 16, 64, 512], P(None, ('groups', 'visit'), 'tile'), parts along dimension 1
The draws below stay inside these ranges and needn't reach their ends.
There are 2 independent parts, one for each index of `groups`. The reference program is written for one: setup_inputs(seed, part) draws one part's arguments, and reference() takes and returns one part's arrays. A program takes and returns all parts, laid end to end along the dimension named above; an argument that names none is the same for every part. Nothing has to cross between parts.
Inputs may be any that keep to these rules, and one draw needn't show every extreme that they name: `stamp_mask`: 1 on the rows of two bands of 16 rows each for every patch and visit (the bands may intersect), 0 elsewhere. `visit_map`: each slot exactly once.
All inputs are finite; a program needn't handle non-finite values.
Results may differ from the reference program's by a relative error of at most 0.0003.
Values sent between devices are 32-bit elements; how exact they have to be, the bound alone decides.
No kernel may reach another device: no remote copies, remote signals or barrier semaphores. Data moves between devices by JAX's collectives and lax.ppermute only.
A program may use at most 64 MiB of HBM per device.

```python
import math
import jax
import jax.numpy as jnp
from jax import lax

COLS = 512
STEPS = 2
BASIS = 40
TAPS = 21
RIM = 10
ROWS = 64
VISITS = 8


def sky_base(key):
    inner = jax.random.fold_in(key, 7001)
    shape = (STEPS, ROWS, COLS)
    return jnp.clip(jax.random.normal(inner, shape, jnp.float32), -5.0, 5.0)


def pixel_noise(key, shape):
    return jnp.clip(jax.random.normal(key, shape, jnp.float32), -5.0, 5.0)


def draw_templates(key, part):
    base = sky_base(key)
    noise = pixel_noise(jax.random.fold_in(key, 7002), (STEPS, VISITS, ROWS, COLS))
    return jnp.clip(base[:, None] + 0.4 * noise, -7.0, 7.0)


def draw_science(key, part):
    base = sky_base(key)
    gains = jnp.exp(jax.random.uniform(jax.random.fold_in(key, 7003), (STEPS, VISITS, 1, 1), jnp.float32, math.log(0.5), math.log(2.0)))
    phases = jax.random.uniform(jax.random.fold_in(key, 7004), (1, VISITS, 1, 1), jnp.float32, 0.0, 2.0 * math.pi)
    rows = jnp.arange(ROWS, dtype=jnp.float32)[None, None, :, None]
    profile = 1.0 + 0.6 * jnp.cos(2.0 * math.pi * rows / ROWS + phases)
    noise = pixel_noise(jax.random.fold_in(key, 7005), (STEPS, VISITS, ROWS, COLS))
    return jnp.clip(gains * profile * base[:, None] + 0.5 * noise, -20.0, 20.0)


def draw_stamp_mask(key, part):
    band = ROWS // 4
    starts = jax.random.randint(jax.random.fold_in(key, 7011), (STEPS, VISITS, 2, 1), 0, ROWS - band + 1)
    rows = jnp.arange(ROWS, dtype=jnp.int32)[None, None, None, :]
    inside = jnp.logical_and(rows >= starts, rows < starts + band).astype(jnp.int32)
    return jnp.max(inside, axis=2)


def basis_profiles(key, salt):
    width = jnp.exp(jax.random.uniform(jax.random.fold_in(key, salt), (BASIS, 1), jnp.float32, math.log(0.7), math.log(3.0)))
    center = jax.random.uniform(jax.random.fold_in(key, salt + 1), (BASIS, 1), jnp.float32, -1.5, 1.5)
    factors = jnp.clip(jax.random.normal(jax.random.fold_in(key, salt + 2), (BASIS, 2), jnp.float32), -3.0, 3.0)
    jitter = jax.random.uniform(jax.random.fold_in(key, salt + 3), (BASIS, TAPS), jnp.float32, -0.5, 0.5)
    offsets = jnp.arange(TAPS, dtype=jnp.float32)[None, :] - RIM
    scaled = (offsets - center) / width
    shaping = 1.0 + 0.5 * factors[:, 0:1] * scaled + 0.3 * factors[:, 1:2] * (scaled * scaled - 1.0)
    return jnp.clip(jnp.exp(-0.5 * scaled * scaled) * shaping + jitter, -3.0, 3.0)


def draw_vertical(key, part):
    return basis_profiles(key, 7021)


def draw_horizontal(key, part):
    return basis_profiles(key, 7031)


def setup_inputs(seed: int = 0, part: int = 0) -> dict:
    seeds = jax.random.split(jax.random.key(seed), 9)
    part_splits = jax.random.split(jax.random.fold_in(seeds[8], part), 9)
    templates = draw_templates(jax.random.fold_in(jax.random.fold_in(seeds[8], part), 71), part)
    science = draw_science(jax.random.fold_in(jax.random.fold_in(seeds[8], part), 71), part)
    stamp_mask = draw_stamp_mask(jax.random.fold_in(jax.random.fold_in(seeds[8], part), 71), part)
    owner = jax.random.randint(part_splits[3], (STEPS,), 0, VISITS).astype(jnp.int32)
    visit_map = jax.random.permutation(part_splits[4], VISITS).astype(jnp.int32)
    vertical = draw_vertical(jax.random.fold_in(seeds[8], 71), part)
    horizontal = draw_horizontal(jax.random.fold_in(seeds[8], 71), part)
    psf = jnp.clip(jax.random.uniform(seeds[7], (TAPS, TAPS), jnp.float32, 0.0, 0.1), 0.0, 0.1)
    return {"templates": templates, "science": science, "stamp_mask": stamp_mask, "owner": owner, "visit_map": visit_map, "vertical": vertical, "horizontal": horizontal, "psf": psf}


RIDGE = 0.05

def tap_stack(piece, tap_count, width):
    return jnp.stack([piece[:, offset:offset + width] for offset in range(tap_count)])

def block_shape(rows, columns):
    row_block = min(rows, 32)
    column_block = min(columns, 512)
    across_count = columns // column_block
    return (row_block, column_block, across_count, rows // row_block * across_count)

def filter_image(extended, kernel):
    tap_count = kernel.shape[1]
    margin = tap_count // 2
    rows = extended.shape[0] - 2 * margin
    columns = extended.shape[1]
    padded = jnp.pad(extended, ((0, 0), (margin, margin)))
    row_block, column_block, across_count, block_count = block_shape(rows, columns)

    def one_block(index, result):
        first_row = index // across_count * row_block
        first_column = index % across_count * column_block
        piece = lax.dynamic_slice(padded, (first_row, first_column), (row_block + 2 * margin, column_block + 2 * margin))
        sideways = jnp.einsum('ij,jyx->iyx', kernel, tap_stack(piece, tap_count, column_block), precision=lax.Precision.HIGHEST)
        total = sideways[0, 0:row_block]
        for offset in range(1, tap_count):
            total = total + sideways[offset, offset:offset + row_block]
        return lax.dynamic_update_slice(result, total, (first_row, first_column))
    return lax.fori_loop(0, block_count, one_block, jnp.zeros((rows, columns), jnp.float32))

def normal_system(extended, image, weights, vertical, horizontal):
    basis_count, tap_count = vertical.shape
    margin = tap_count // 2
    rows, columns = image.shape
    padded = jnp.pad(extended, ((0, 0), (margin, margin)))
    row_block, column_block, across_count, block_count = block_shape(rows, columns)

    def one_block(index, totals):
        matrix, vector = totals
        first_row = index // across_count * row_block
        first_column = index % across_count * column_block
        piece = lax.dynamic_slice(padded, (first_row, first_column), (row_block + 2 * margin, column_block + 2 * margin))
        sideways = jnp.einsum('kj,jyx->kyx', horizontal, tap_stack(piece, tap_count, column_block), precision=lax.Precision.HIGHEST)
        convolved = vertical[:, 0, None, None] * sideways[:, 0:row_block]
        for offset in range(1, tap_count):
            convolved = convolved + vertical[:, offset, None, None] * sideways[:, offset:offset + row_block]
        chosen = lax.dynamic_slice_in_dim(weights, first_row, row_block).astype(jnp.float32)
        observed = lax.dynamic_slice(image, (first_row, first_column), (row_block, column_block))
        flat = convolved.reshape(basis_count, -1)
        weighted = (convolved * chosen[None, :, None]).reshape(basis_count, -1)
        matrix = matrix + lax.dot_general(weighted, flat, (((1,), (1,)), ((), ())), precision=lax.Precision.HIGHEST)
        vector = vector + jnp.dot(weighted, observed.reshape(-1), precision=lax.Precision.HIGHEST)
        return (matrix, vector)
    start = (jnp.zeros((basis_count, basis_count), jnp.float32), jnp.zeros((basis_count,), jnp.float32))
    return lax.fori_loop(0, block_count, one_block, start)

def solve_kernel(matrix, vector, vertical, horizontal):
    basis_count = matrix.shape[0]
    regular = matrix + RIDGE * jnp.trace(matrix) / basis_count * jnp.eye(basis_count, dtype=jnp.float32)
    factor = jnp.linalg.cholesky(regular)
    coefficients = jax.scipy.linalg.cho_solve((factor, True), vector)
    return jnp.einsum('k,ki,kj->ij', coefficients, vertical, horizontal, precision=lax.Precision.HIGHEST)

def reference(templates, science, stamp_mask, owner, visit_map, vertical, horizontal, psf):
    margin = vertical.shape[1] // 2
    differences = []
    likelihoods = []
    for step in range(STEPS):
        slot = visit_map[owner[step].astype(jnp.int32)].astype(jnp.int32)
        template = lax.dynamic_index_in_dim(templates[step], slot, 0, keepdims=False)
        extended = jnp.pad(template, ((margin, margin), (0, 0)))

        def one_visit(inputs, extended=extended):
            image, weights = inputs
            matrix, vector = normal_system(extended, image, weights, vertical, horizontal)
            kernel = solve_kernel(matrix, vector, vertical, horizontal)
            difference = image - filter_image(extended, kernel)
            likelihood = filter_image(jnp.pad(difference, ((margin, margin), (0, 0))), psf)
            return (difference, likelihood)
        difference, likelihood = lax.map(one_visit, (science[step], stamp_mask[step]))
        differences.append(difference)
        likelihoods.append(likelihood)
    return (jnp.stack(differences), jnp.stack(likelihoods))
```

```python
import jax
import jax.numpy as jnp
from jax import lax
from jax.experimental import pallas as pl
from jax.experimental.pallas import tpu as pltpu
from jax.sharding import PartitionSpec as P

RIDGE = 0.05
F32 = jnp.float32
BF16 = jnp.bfloat16
HIGHEST = lax.Precision.HIGHEST
NN = (((1,), (0,)), ((), ()))
NT = (((1,), (1,)), ((), ()))
TN = (((0,), (0,)), ((), ()))

LANES = 128
GROUP = 64
SHIFTS = 4
STRIDES = 6
CROSS = 3
EDGE_TAPS = 6
TAP_PAD = 32
START = 43


def iota(shape, dim):
    return lax.broadcasted_iota(jnp.int32, shape, dim)


def split(x):
    high = x.astype(BF16)
    return high, (x - high.astype(F32)).astype(BF16)


def dot(a, b, dims):
    return lax.dot_general(a, b, dims, preferred_element_type=F32)


def dot3(a, b, dims):
    return dot(a[0], b[0], dims) + (dot(a[0], b[1], dims) + dot(a[1], b[0], dims))


def exact(a, b, dims):
    return lax.dot_general(a, b, dims, precision=HIGHEST, preferred_element_type=F32)


def shift_right(x, amount):
    if amount == 0:
        return x
    return jnp.where(iota(x.shape, 1) >= amount, pltpu.roll(x, amount, 1), 0.0)


def shift_left(x, amount):
    if amount == 0:
        return x
    width = x.shape[1]
    return jnp.where(iota(x.shape, 1) < width - amount, pltpu.roll(x, width - amount, 1), 0.0)


def flip_rows(x):
    count = x.shape[0]
    mirror = iota((count, count), 0) + iota((count, count), 1) == count - 1
    return exact(mirror.astype(F32), x, NN)


def store_split(refs, index, x):
    high, low = split(x)
    refs[0][index] = high
    refs[1][index] = low


def write_bands(reverse, taps, refs):
    row = iota((LANES, LANES), 0)
    lane = iota((LANES, LANES), 1)
    for ref in refs:
        ref[LANES:, :] = jnp.zeros((LANES, ref.shape[1]), BF16)
        ref[:LANES, taps * LANES :] = jnp.zeros((LANES, ref.shape[1] - taps * LANES), BF16)
    for tap in range(taps):
        base = jnp.broadcast_to(reverse[tap : tap + 1, :], (LANES, LANES))
        turned = pltpu.roll(base, 0, 1, stride=1, stride_axis=0)
        here = slice(tap * LANES, (tap + 1) * LANES)
        store_split(refs, (slice(0, LANES), here), jnp.where(lane <= row, turned, 0.0))
        store_split(
            refs,
            (slice(LANES, LANES + 32), here),
            jnp.where(lane[:32] > row[:32], turned[:32], 0.0),
        )


def prepare(
    tile_ref, vertical_ref, horizontal_ref, psf_ref, own_ref, other_ref, mask_ref, mask_other_ref,
    vb_high, vb_low, vq_ref, hc_ref, vh_ref, edge_high, edge_low, hrev_ref, vpad_ref,
    band_high, band_low, left_high, left_low, right_high, right_low, rows_ref, lane_ref,
    v_pad, h_pad, h_wide, psf_pad, science, chosen,
):
    basis, taps = vertical_ref.shape
    steps = own_ref.shape[0]
    rim = taps // 2
    half = own_ref.shape[2]
    tile = tile_ref[0]
    v_pad[...] = jnp.zeros(v_pad.shape, F32)
    h_pad[...] = jnp.zeros(h_pad.shape, F32)
    h_wide[...] = jnp.zeros(h_wide.shape, F32)
    psf_pad[...] = jnp.zeros(psf_pad.shape, F32)
    v_pad[:basis, :taps] = vertical_ref[...]
    h_pad[:basis, :taps] = horizontal_ref[...]
    h_wide[:basis, :taps] = horizontal_ref[...]
    psf_pad[:taps, :taps] = psf_ref[...]
    v_all = v_pad[...]
    v = v_all[:basis]
    h = h_pad[:basis]
    wide = SHIFTS * GROUP

    def pick(width, index):
        return (iota((TAP_PAD, width), 0) == index).astype(F32)

    lane = (iota((TAP_PAD, wide), 1) + wide - START) % wide
    turn, place = lane // GROUP, lane % GROUP

    def source(shape):
        return (iota(shape, 0) + wide - START - TAP_PAD + 1) % wide

    select = 2 * rim - source((wide, TAP_PAD)) % GROUP == iota((wide, TAP_PAD), 1)
    every = exact(select.astype(F32), jnp.concatenate([v_all] * SHIFTS, axis=0), NT)
    same = source((wide, wide)) // GROUP == iota((wide, wide), 1) // GROUP
    store_split((vb_high, vb_low), (slice(None), slice(None)), jnp.where(same, every, 0.0))

    mirror = iota((TAP_PAD, TAP_PAD), 0) + iota((TAP_PAD, TAP_PAD), 1) == TAP_PAD - 1
    v_high, v_low = split(exact(v, mirror.astype(F32), NN))
    vq_ref[:, 0:TAP_PAD] = v_high
    vq_ref[:, TAP_PAD : 2 * TAP_PAD] = v_high
    vq_ref[:, 2 * TAP_PAD : 3 * TAP_PAD] = v_low

    h_all = h_wide[...]
    for q in range(STRIDES):
        pieces = []
        for s in range(SHIFTS):
            distance = SHIFTS * q + s
            pieces.append(pltpu.roll(h_all, (LANES - distance) % LANES, 1))
        both = exact(h_all[:basis], jnp.concatenate(pieces, axis=0), NT)
        if q == 0:
            both = jnp.where(iota(both.shape, 1) < GROUP, 0.5 * both, both)
        hc_ref[q] = both

    down = exact(v, pick(wide, 3 * rim - place), NN)
    up = exact(v, pick(wide, place - rim), NN)
    for q in range(CROSS):
        ahead = exact(h, pick(wide, rim + SHIFTS * q + turn), NN)
        behind = exact(h, pick(wide, rim - SHIFTS * q - turn), NN)
        if q == 0:
            behind = jnp.where(turn[:1] == 0, 0.0, behind)
        vh_ref[q] = down * ahead
        vh_ref[CROSS + q] = up * behind

    narrow = iota((TAP_PAD, LANES), 1)
    part = narrow // (2 * rim)
    column = narrow % (2 * rim)
    used = part < EDGE_TAPS
    spread_v = jnp.concatenate(
        [
            exact(v, pick(LANES, jnp.where(used, EDGE_TAPS * t + part, -1)), NN)
            for t in range(4)
        ],
        axis=1,
    )
    for e in range(2 * rim):
        offset = 2 * rim - e if e < rim else -e
        spread_h = exact(h, pick(LANES, jnp.where(used, column + offset, -1)), NN)
        store_split(
            (edge_high, edge_low),
            (slice(e * basis, (e + 1) * basis), slice(None)),
            spread_v * jnp.concatenate([spread_h] * 4, axis=1),
        )

    back = pick(LANES, (LANES - narrow) % LANES)
    hrev_ref[...] = exact(h, back, NN)
    vpad_ref[...] = jnp.zeros(vpad_ref.shape, F32)
    vpad_ref[:, :TAP_PAD] = v
    write_bands(exact(psf_pad[...], back, NN), taps, (band_high, band_low))

    for step in range(steps):
        science[pl.ds(half * tile, half), :] = own_ref[step, 0]
        science[pl.ds(half * (1 - tile), half), :] = other_ref[step, 0]
        first = jnp.where(tile == 0, mask_ref[step], mask_other_ref[step]).astype(F32)
        second = jnp.where(tile == 0, mask_other_ref[step], mask_ref[step]).astype(F32)
        mask = jnp.concatenate([first, second], axis=1)
        diagonal = iota((GROUP, GROUP), 0) == iota((GROUP, GROUP), 1)
        column_mask = jnp.sum(jnp.where(diagonal, mask, 0.0), axis=1, keepdims=True)
        masked = science[...] * column_mask
        mirrored = flip_rows(masked)
        for q in range(CROSS):
            store_split(
                (left_high, left_low),
                (step, slice(q * GROUP, (q + 1) * GROUP), slice(None)),
                shift_right(masked, SHIFTS * q),
            )
        for s in range(SHIFTS):
            store_split(
                (right_high, right_low),
                (step, slice(s * GROUP, (s + 1) * GROUP), slice(None)),
                shift_left(mirrored, s),
            )
        chosen[...] = jnp.zeros(chosen.shape, F32)
        single = jnp.concatenate([mask, jnp.zeros((1, GROUP), F32)], axis=1)
        for tap in range(taps):
            place_row = TAP_PAD - 1 - tap
            chosen[place_row : place_row + 1, :] = pltpu.roll(single, (tap - rim) % LANES, 1)
        moved = chosen[...][:, :GROUP]
        rows_ref[step] = jnp.concatenate([moved, moved], axis=1).astype(BF16)
        zero = jnp.zeros((1, GROUP), F32)
        ordered = [zero] * steps
        ordered[step] = mask
        lane_ref[step] = jnp.concatenate(ordered, axis=1)


def solve(system):
    count = system.shape[0]
    row = iota(system.shape, 0)
    for pivot in range(count):
        scaled = system[pivot : pivot + 1, :] / system[pivot : pivot + 1, pivot : pivot + 1]
        reduced = system - system[:, pivot : pivot + 1] * scaled
        system = jnp.where(row == pivot, scaled, reduced)
    return system[:, count : count + 1]


def apply_bands(image, band_refs, sums, rows, taps, start, out_rows):
    block_count = (image[0].shape[1] - LANES) // LANES
    left = [
        jnp.concatenate(
            [piece[:, c * LANES : (c + 2) * LANES] for c in range(block_count)], axis=0
        )
        for piece in image
    ]
    for pair in range((taps + 1) // 2):
        here = slice(pair * 2 * LANES, (pair + 1) * 2 * LANES)
        both = dot3(left, [ref[:, here] for ref in band_refs], NN)
        for side in range(2):
            if 2 * pair + side < taps:
                sums[2 * pair + side, : block_count * rows, :] = both[:, side * LANES : (side + 1) * LANES]
    blocks = []
    for c in range(block_count):
        total = None
        for tap in range(taps):
            first = c * rows + start + tap
            term = sums[tap, first : first + out_rows, :]
            total = term if total is None else total + term
        blocks.append(total)
    return jnp.concatenate(blocks, axis=1)


def fit(
    tile_ref, own_ref, other_ref, science_ref, science_other_ref,
    vb_high, vb_low, vq_ref, hc_ref, vh_ref, edge_high, edge_low, hrev_ref, vpad_ref,
    band_high, band_low, left_high, left_low, right_high, right_low, rows_ref, lane_ref,
    difference_ref, likelihood_ref,
    template, science, border, wide_high, wide_low, kernel_high, kernel_low,
    sums, window, tall_high, tall_low,
):
    steps = own_ref.shape[0]
    half = own_ref.shape[2]
    columns = own_ref.shape[3]
    basis = hrev_ref.shape[0]
    taps = 21
    rim = taps // 2
    tile = tile_ref[0]
    wide = SHIFTS * GROUP
    place = (iota((GROUP, wide), 1) + wide - START) % wide % GROUP
    other_row = iota((GROUP, wide), 0) + 2 * rim - place
    valid = (other_row >= 0) & (other_row < GROUP) & (place <= 4 * rim)
    totals = []
    vectors = []
    stacks = []
    border[...] = jnp.zeros(border.shape, F32)
    wide_high[...] = jnp.zeros(wide_high.shape, BF16)
    wide_low[...] = jnp.zeros(wide_low.shape, BF16)
    for step in range(steps):
        template[pl.ds(half * tile, half), :] = own_ref[step, 0]
        template[pl.ds(half * (1 - tile), half), :] = other_ref[step, 0]
        image = template[...]
        mirrored = flip_rows(image)
        left = [[], []]
        for q in range(STRIDES):
            for side, piece in enumerate(split(shift_right(image, SHIFTS * q))):
                left[side].append(piece)
        left = [jnp.concatenate(pieces, axis=0) for pieces in left]
        right = [[], []]
        for s in range(SHIFTS):
            for side, piece in enumerate(split(shift_left(mirrored, s))):
                right[side].append(piece)
        right = [jnp.concatenate(pieces, axis=0) for pieces in right]
        auto = dot3(left, right, NT)
        ahead = dot3((left_high[step], left_low[step]), right, NT)
        near = [piece[: CROSS * GROUP] for piece in left]
        behind = dot3(near, (right_high[step], right_low[step]), NT)

        def align(block):
            turned = pltpu.roll(block, 0, 1, stride=1, stride_axis=0)
            return jnp.where(valid, turned, 0.0)

        weights = rows_ref[step]
        products = []
        for q in range(STRIDES):
            high, low = split(align(auto[q * GROUP : (q + 1) * GROUP]))
            gathered = dot(weights, jnp.concatenate([high, low], axis=0), NN)
            products.append(pltpu.roll(gathered, 0, 1, stride=1, stride_axis=0))
        partial = dot3(split(jnp.concatenate(products, axis=0)), (vb_high[...], vb_low[...]), NN)
        total = None
        for q in range(STRIDES):
            high, low = split(partial[q * TAP_PAD : (q + 1) * TAP_PAD])
            mixed = dot(vq_ref[...], jnp.concatenate([high, low, high], axis=0), NN)
            term = mixed * hc_ref[q]
            total = term if total is None else total + term
        total = total[:, :LANES] + total[:, LANES:]
        totals.append(total + pltpu.roll(total, GROUP, 1))

        vector = None
        for q in range(CROSS):
            here = slice(q * GROUP, (q + 1) * GROUP)
            for index, block in ((q, ahead), (CROSS + q, behind)):
                row = jnp.sum(align(block[here]), axis=0, keepdims=True)
                term = vh_ref[index] * row
                vector = term if vector is None else vector + term
        vectors.append(jnp.sum(vector, axis=1, keepdims=True))

        lane = iota((GROUP, LANES), 1)
        far = pltpu.roll(image[:, columns - LANES :], 2 * rim, 1)
        border[16 : 16 + GROUP, :] = jnp.where(
            lane < rim, image[:, :LANES], jnp.where(lane < 2 * rim, far, 0.0)
        )
        chunks = []
        for t in range(4):
            chunk = None
            for g in range(EDGE_TAPS):
                tap = EDGE_TAPS * t + g
                if tap < taps:
                    piece = border[tap + 16 - rim : tap + 16 - rim + GROUP, :]
                    piece = pltpu.roll(piece, 2 * rim * g, 1) if g else piece
                    chunk = piece if chunk is None else chunk + piece
            chunks.append(chunk)
        stacks.append(jnp.concatenate(chunks, axis=1))

        padded = pltpu.roll(
            jnp.concatenate([image, jnp.zeros((GROUP, LANES), F32)], axis=1), rim, 1
        )
        store_split((wide_high, wide_low), (step, slice(16, 16 + GROUP), slice(None)), padded)

    stack = split(jnp.concatenate(stacks, axis=0))
    outside = dot3((edge_high[...], edge_low[...]), stack, NT)
    outside = jnp.concatenate(
        [outside[e * basis : (e + 1) * basis] for e in range(2 * rim)], axis=1
    )
    out_high, out_low = split(outside)

    row = iota((basis, LANES), 0)
    lane = iota((basis, LANES), 1)
    for step in range(steps):
        keep = jnp.concatenate([lane_ref[step]] * (2 * rim), axis=1)
        kept_high, kept_low = split(outside * keep)
        removed = dot3((kept_high, kept_low), (out_high, out_low), NT)
        square = jnp.concatenate(
            [totals[step], jnp.zeros((LANES - basis, LANES), F32)], axis=0
        )
        matrix = (square + square.T)[:basis]
        removed = jnp.concatenate([removed, jnp.zeros((basis, LANES - basis), F32)], axis=1)
        matrix = jnp.where(lane < basis, matrix - removed, 0.0)
        trace = jnp.sum(jnp.where(row == lane, matrix, 0.0), keepdims=True)
        system = jnp.where(row == lane, matrix + RIDGE * trace / basis, matrix)
        system = jnp.where(lane == basis, vectors[step], system)
        coefficients = solve(system)
        reverse = exact(coefficients * vpad_ref[...], hrev_ref[...], TN)
        write_bands(reverse, taps, (kernel_high, kernel_low))
        view = (step, pl.ds(pl.multiple_of(16 * tile, 16), 80), slice(None))
        modelled = apply_bands(
            (wide_high[view], wide_low[view]), (kernel_high, kernel_low), sums, 80, taps, 6, 48
        )
        science[pl.ds(half * tile, half), :] = science_ref[step, 0]
        science[pl.ds(half * (1 - tile), half), :] = science_other_ref[step, 0]
        found = science[pl.ds(pl.multiple_of(16 * tile, 16), 48), :] - modelled
        window[...] = found
        difference_ref[step, 0] = window[pl.ds(pl.multiple_of(16 * tile, 16), half), :]
        padded = pltpu.roll(
            jnp.concatenate([found, jnp.zeros((48, LANES), F32)], axis=1), rim, 1
        )
        for ref in (tall_high, tall_low):
            ref[0:16, :] = jnp.zeros((16, ref.shape[1]), BF16)
            ref[64:80, :] = jnp.zeros((16, ref.shape[1]), BF16)
        store_split((tall_high, tall_low), (slice(16, 64), slice(None)), padded)
        view = (pl.ds(pl.multiple_of(16 * tile, 16), 64), slice(None))
        likelihood_ref[step, 0] = apply_bands(
            (tall_high[view], tall_low[view]), (band_high, band_low), sums, 64, taps, 6, half
        )


def in_vmem(count):
    return [pl.BlockSpec(memory_space=pltpu.VMEM)] * count


def in_smem(count):
    return [pl.BlockSpec(memory_space=pltpu.SMEM)] * count


def run_prepare(tile, vertical, horizontal, psf, own, other, mask, mask_other):
    basis, taps = vertical.shape
    steps, _, half, columns = own.shape
    wide = SHIFTS * GROUP
    shapes = [
        ((wide, wide), BF16), ((wide, wide), BF16),
        ((basis, 3 * TAP_PAD), BF16),
        ((STRIDES, basis, wide), F32),
        ((2 * CROSS, basis, wide), F32),
        ((2 * (taps // 2) * basis, 4 * LANES), BF16), ((2 * (taps // 2) * basis, 4 * LANES), BF16),
        ((basis, LANES), F32), ((basis, LANES), F32),
        ((2 * LANES, (taps + 1) * LANES), BF16), ((2 * LANES, (taps + 1) * LANES), BF16),
        ((steps, CROSS * GROUP, columns), BF16), ((steps, CROSS * GROUP, columns), BF16),
        ((steps, wide, columns), BF16), ((steps, wide, columns), BF16),
        ((steps, TAP_PAD, 2 * GROUP), BF16),
        ((steps, 1, LANES), F32),
    ]
    return pl.pallas_call(
        prepare,
        out_shape=[jax.ShapeDtypeStruct(shape, dtype) for shape, dtype in shapes],
        in_specs=in_smem(1) + in_vmem(7),
        out_specs=in_vmem(len(shapes)),
        scratch_shapes=[
            pltpu.VMEM((GROUP, TAP_PAD), F32),
            pltpu.VMEM((GROUP, TAP_PAD), F32),
            pltpu.VMEM((GROUP, LANES), F32),
            pltpu.VMEM((TAP_PAD, TAP_PAD), F32),
            pltpu.VMEM((GROUP, columns), F32),
            pltpu.VMEM((TAP_PAD, LANES), F32),
        ],
        compiler_params=pltpu.CompilerParams(vmem_limit_bytes=24 << 20),
        cost_estimate=pl.CostEstimate(flops=4_000_000_000, bytes_accessed=8_000_000, transcendentals=0),
        name="prepare",
    )(tile, vertical, horizontal, psf, own, other, mask, mask_other)


def run_fit(tile, own, other, science, science_other, prepared, taps):
    steps, _, half, columns = own.shape
    padded = columns + LANES
    return pl.pallas_call(
        fit,
        out_shape=[jax.ShapeDtypeStruct(own.shape, F32)] * 2,
        in_specs=in_smem(1) + in_vmem(4 + len(prepared)),
        out_specs=in_vmem(2),
        scratch_shapes=[
            pltpu.VMEM((GROUP, columns), F32),
            pltpu.VMEM((GROUP, columns), F32),
            pltpu.VMEM((GROUP + 32, LANES), F32),
            pltpu.VMEM((steps, GROUP + 32, padded), BF16),
            pltpu.VMEM((steps, GROUP + 32, padded), BF16),
            pltpu.VMEM((2 * LANES, (taps + 1) * LANES), BF16),
            pltpu.VMEM((2 * LANES, (taps + 1) * LANES), BF16),
            pltpu.VMEM((taps, 4 * 80, LANES), F32),
            pltpu.VMEM((48, columns), F32),
            pltpu.VMEM((80, padded), BF16),
            pltpu.VMEM((80, padded), BF16),
        ],
        compiler_params=pltpu.CompilerParams(vmem_limit_bytes=32 << 20),
        cost_estimate=pl.CostEstimate(flops=20_000_000_000, bytes_accessed=16_000_000, transcendentals=0),
        name="fit",
    )(tile, own, other, science, science_other, *prepared)


def spread(templates, owner, visit_map):
    count = lax.axis_size("visit")
    steps = templates.shape[0]
    distance = jnp.bitwise_xor(visit_map[owner], lax.axis_index("visit"))
    seen = 0
    block = templates
    bit = 1
    while bit < count:
        arrived = lax.ppermute(block, "visit", [(i, i ^ bit) for i in range(count)])
        holds = jnp.bitwise_and(distance, (count - 1) & ~seen) == 0
        block = jnp.where(holds.reshape(steps, 1, 1, 1), block, arrived)
        seen |= bit
        bit *= 2
    return block


def on_device(templates, science, stamp_mask, owner, visit_map, vertical, horizontal, psf):
    swap = [(0, 1), (1, 0)]
    tile = lax.axis_index("tile").astype(jnp.int32).reshape(1)
    science_other = lax.ppermute(science, "tile", swap)
    mask_other = lax.ppermute(stamp_mask, "tile", swap)
    prepared = run_prepare(
        tile, vertical, horizontal, psf, science, science_other, stamp_mask, mask_other
    )
    template = spread(templates, owner, visit_map)
    template_other = lax.ppermute(template, "tile", swap)
    return tuple(
        run_fit(
            tile, template, template_other, science, science_other, prepared, vertical.shape[1]
        )
    )


def solution(mesh):
    placed = (
        P(None, ("groups", "visit"), "tile", None),
        P(None, ("groups", "visit"), "tile", None),
        P(None, ("groups", "visit"), "tile"),
        P("groups"),
        P("groups"),
        P(),
        P(),
        P(),
    )
    return jax.shard_map(
        on_device,
        mesh=mesh,
        in_specs=placed,
        out_specs=(
            P(None, ("groups", "visit"), "tile", None),
            P(None, ("groups", "visit"), "tile", None),
        ),
        check_vma=False,
    )
```

```python
import jax
import jax.numpy as jnp
from jax import lax
from jax.experimental import pallas as pl
from jax.experimental.pallas import tpu as pltpu
from jax.sharding import PartitionSpec as P

RIDGE = 0.05
F32 = jnp.float32
BF16 = jnp.bfloat16
HIGHEST = lax.Precision.HIGHEST
NN = (((1,), (0,)), ((), ()))
NT = (((1,), (1,)), ((), ()))
TN = (((0,), (0,)), ((), ()))

LANES = 128
GROUP = 64
SHIFTS = 4
STRIDES = 6
CROSS = 3
EDGE_TAPS = 6
TAP_PAD = 32
REST = 32
PANEL = 8
MARGIN = 16
START = 43


def iota(shape, dim):
    return lax.broadcasted_iota(jnp.int32, shape, dim)


def split(x):
    high = x.astype(BF16)
    return high, (x - high.astype(F32)).astype(BF16)


def dot(a, b, dims):
    return lax.dot_general(a, b, dims, preferred_element_type=F32)


def dot3(a, b, dims):
    return dot(a[0], b[0], dims) + (dot(a[0], b[1], dims) + dot(a[1], b[0], dims))


def exact(a, b, dims):
    return lax.dot_general(a, b, dims, precision=HIGHEST, preferred_element_type=F32)


def shift_right(x, amount):
    if amount == 0:
        return x
    return jnp.where(iota(x.shape, 1) >= amount, pltpu.roll(x, amount, 1), 0.0)


def shift_left(x, amount):
    if amount == 0:
        return x
    width = x.shape[1]
    return jnp.where(iota(x.shape, 1) < width - amount, pltpu.roll(x, width - amount, 1), 0.0)


def flip_rows(x):
    count = x.shape[0]
    mirror = iota((count, count), 0) + iota((count, count), 1) == count - 1
    return exact(mirror.astype(F32), x, NN)


def store_split(refs, index, x):
    high, low = split(x)
    refs[0][index] = high
    refs[1][index] = low


def write_bands(reverse, taps, ref):
    row = iota((LANES, LANES), 0)
    lane = iota((LANES, LANES), 1)
    ref[3 * LANES + 3 * REST :, :] = jnp.zeros((LANES - 3 * REST, ref.shape[1]), BF16)
    ref[:, taps * LANES :] = jnp.zeros((ref.shape[0], ref.shape[1] - taps * LANES), BF16)
    for tap in range(taps):
        base = jnp.broadcast_to(reverse[tap : tap + 1, :], (LANES, LANES))
        turned = pltpu.roll(base, 0, 1, stride=1, stride_axis=0)
        here = slice(tap * LANES, (tap + 1) * LANES)
        high, low = split(jnp.where(lane <= row, turned, 0.0))
        ref[0:LANES, here] = high
        ref[LANES : 2 * LANES, here] = high
        ref[2 * LANES : 3 * LANES, here] = low
        high, low = split(jnp.where(lane[:REST] > row[:REST], turned[:REST], 0.0))
        ref[3 * LANES : 3 * LANES + REST, here] = high
        ref[3 * LANES + REST : 3 * LANES + 2 * REST, here] = high
        ref[3 * LANES + 2 * REST : 3 * LANES + 3 * REST, here] = low


def prepare(
    tile_ref, vertical_ref, horizontal_ref, psf_ref, own_ref, other_ref, mask_ref, mask_other_ref,
    vb_high, vb_low, vq_ref, hc_ref, vh_ref, edge_high, edge_low, hrev_ref, vpad_ref,
    band_ref, left_high, left_low, right_high, right_low, rows_ref, lane_ref, target_ref,
    v_pad, h_pad, h_wide, psf_pad, science, chosen,
):
    basis, taps = vertical_ref.shape
    steps = own_ref.shape[0]
    rim = taps // 2
    half = own_ref.shape[2]
    tile = tile_ref[0]
    v_pad[...] = jnp.zeros(v_pad.shape, F32)
    h_pad[...] = jnp.zeros(h_pad.shape, F32)
    h_wide[...] = jnp.zeros(h_wide.shape, F32)
    psf_pad[...] = jnp.zeros(psf_pad.shape, F32)
    v_pad[:basis, :taps] = vertical_ref[...]
    h_pad[:basis, :taps] = horizontal_ref[...]
    h_wide[:basis, :taps] = horizontal_ref[...]
    psf_pad[:taps, :taps] = psf_ref[...]
    v_all = v_pad[...]
    v = v_all[:basis]
    h = h_pad[:basis]
    wide = SHIFTS * GROUP

    def pick(width, index):
        return (iota((TAP_PAD, width), 0) == index).astype(F32)

    lane = (iota((TAP_PAD, wide), 1) + wide - START) % wide
    turn, place = lane // GROUP, lane % GROUP

    def source(shape):
        return (iota(shape, 0) + wide - START - TAP_PAD + 1) % wide

    select = 2 * rim - source((wide, TAP_PAD)) % GROUP == iota((wide, TAP_PAD), 1)
    every = exact(select.astype(F32), jnp.concatenate([v_all] * SHIFTS, axis=0), NT)
    same = source((wide, wide)) // GROUP == iota((wide, wide), 1) // GROUP
    store_split((vb_high, vb_low), (slice(None), slice(None)), jnp.where(same, every, 0.0))

    mirror = iota((TAP_PAD, TAP_PAD), 0) + iota((TAP_PAD, TAP_PAD), 1) == TAP_PAD - 1
    v_high, v_low = split(exact(v, mirror.astype(F32), NN))
    vq_ref[:, 0:TAP_PAD] = v_high
    vq_ref[:, TAP_PAD : 2 * TAP_PAD] = v_high
    vq_ref[:, 2 * TAP_PAD : 3 * TAP_PAD] = v_low

    h_all = h_wide[...]
    for q in range(STRIDES):
        pieces = []
        for s in range(SHIFTS):
            distance = SHIFTS * q + s
            pieces.append(pltpu.roll(h_all, (LANES - distance) % LANES, 1))
        both = exact(h_all[:basis], jnp.concatenate(pieces, axis=0), NT)
        if q == 0:
            both = jnp.where(iota(both.shape, 1) < GROUP, 0.5 * both, both)
        hc_ref[q] = both

    down = exact(v, pick(wide, 3 * rim - place), NN)
    up = exact(v, pick(wide, place - rim), NN)
    for q in range(CROSS):
        ahead = exact(h, pick(wide, rim + SHIFTS * q + turn), NN)
        behind = exact(h, pick(wide, rim - SHIFTS * q - turn), NN)
        if q == 0:
            behind = jnp.where(turn[:1] == 0, 0.0, behind)
        vh_ref[q] = down * ahead
        vh_ref[CROSS + q] = up * behind

    narrow = iota((TAP_PAD, LANES), 1)
    part = narrow // (2 * rim)
    column = narrow % (2 * rim)
    used = part < EDGE_TAPS
    spread_v = jnp.concatenate(
        [
            exact(v, pick(LANES, jnp.where(used, EDGE_TAPS * t + part, -1)), NN)
            for t in range(4)
        ],
        axis=1,
    )
    for e in range(2 * rim):
        offset = 2 * rim - e if e < rim else -e
        spread_h = exact(h, pick(LANES, jnp.where(used, column + offset, -1)), NN)
        store_split(
            (edge_high, edge_low),
            (slice(e * basis, (e + 1) * basis), slice(None)),
            spread_v * jnp.concatenate([spread_h] * 4, axis=1),
        )

    back = pick(LANES, (LANES - narrow) % LANES)
    hrev_ref[...] = exact(h, back, NN)
    vpad_ref[...] = jnp.zeros(vpad_ref.shape, F32)
    vpad_ref[:, :TAP_PAD] = v
    write_bands(exact(psf_pad[...], back, NN), taps, band_ref)

    for step in range(steps):
        science[pl.ds(half * tile, half), :] = own_ref[step, 0]
        science[pl.ds(half * (1 - tile), half), :] = other_ref[step, 0]
        first = jnp.where(tile == 0, mask_ref[step], mask_other_ref[step]).astype(F32)
        second = jnp.where(tile == 0, mask_other_ref[step], mask_ref[step]).astype(F32)
        mask = jnp.concatenate([first, second], axis=1)
        diagonal = iota((GROUP, GROUP), 0) == iota((GROUP, GROUP), 1)
        column_mask = jnp.sum(jnp.where(diagonal, mask, 0.0), axis=1, keepdims=True)
        masked = science[...] * column_mask
        mirrored = flip_rows(masked)
        for q in range(CROSS):
            store_split(
                (left_high, left_low),
                (step, slice(q * GROUP, (q + 1) * GROUP), slice(None)),
                shift_right(masked, SHIFTS * q),
            )
        for s in range(SHIFTS):
            store_split(
                (right_high, right_low),
                (step, slice(s * GROUP, (s + 1) * GROUP), slice(None)),
                shift_left(mirrored, s),
            )
        chosen[...] = jnp.zeros(chosen.shape, F32)
        single = jnp.concatenate([mask, jnp.zeros((1, GROUP), F32)], axis=1)
        for tap in range(taps):
            place_row = TAP_PAD - 1 - tap
            chosen[place_row : place_row + 1, :] = pltpu.roll(single, (tap - rim) % LANES, 1)
        moved = chosen[...][:, :GROUP]
        rows_ref[step] = jnp.concatenate([moved, moved], axis=1).astype(BF16)
        zero = jnp.zeros((1, GROUP), F32)
        ordered = [zero] * steps
        ordered[step] = mask
        lane_ref[step] = jnp.concatenate(ordered, axis=1)
        target_ref[step] = jnp.where(
            tile == 0, science[0 : half + rim, :], science[half - rim : 2 * half, :]
        )


def solve(systems):
    count, width = systems[0].shape
    row = iota((count, width), 0)
    lane = iota((count, width), 1)
    for first in range(0, count, PANEL):
        panels = [
            [
                jnp.broadcast_to(system[:, first + j : first + j + 1], (count, width))
                for j in range(PANEL)
            ]
            for system in systems
        ]
        for j in range(PANEL):
            pivot = first + j
            for index, panel in enumerate(panels):
                column = panel[j]
                factor = column * (1.0 / column[pivot : pivot + 1, :])
                factor = jnp.where(row == pivot, 0.0, factor)
                for m in range(j + 1, PANEL):
                    panel[m] = panel[m] - factor * panel[m][pivot : pivot + 1, :]
                system = systems[index]
                systems[index] = system - factor * system[pivot : pivot + 1, :]
    results = []
    for system in systems:
        scale = jnp.sum(jnp.where(row == lane, system, 0.0), axis=1, keepdims=True)
        results.append(system[:, count : count + 1] / scale)
    return results


def columns_for_bands(image, rim):
    rows, columns = image.shape
    padded = pltpu.roll(
        jnp.concatenate([image, jnp.zeros((rows, LANES), F32)], axis=1), rim, 1
    )
    high, low = split(padded)
    lane = iota((rows, LANES), 1)
    blocks = []
    for c in range(columns // LANES):
        here = slice(c * LANES, (c + 1) * LANES)
        there = slice((c + 1) * LANES, (c + 2) * LANES)
        next_high = high[:, there].astype(F32)
        next_low = low[:, there].astype(F32)
        rest = jnp.where(
            lane < REST,
            next_high,
            jnp.where(
                lane < 2 * REST,
                pltpu.roll(next_low, REST, 1),
                jnp.where(lane < 3 * REST, pltpu.roll(next_high, 2 * REST, 1), 0.0),
            ),
        )
        blocks.append(
            jnp.concatenate([high[:, here], low[:, here], high[:, here], rest.astype(BF16)], axis=1)
        )
    return jnp.concatenate(blocks, axis=0)


def apply_bands(left, band_ref, sums, rows, taps, out_rows):
    block_count = left.shape[0] // rows
    for pair in range((taps + 1) // 2):
        both = dot(left, band_ref[:, pair * 2 * LANES : (pair + 1) * 2 * LANES], NN)
        for side in range(2):
            if 2 * pair + side < taps:
                sums[2 * pair + side] = both[:, side * LANES : (side + 1) * LANES]
    blocks = []
    for c in range(block_count):
        total = None
        for tap in range(taps):
            first = c * rows + tap
            term = sums[tap, first : first + out_rows, :]
            total = term if total is None else total + term
        blocks.append(total)
    return jnp.concatenate(blocks, axis=1)


def fit(
    tile_ref, own_ref, other_ref,
    vb_high, vb_low, vq_ref, hc_ref, vh_ref, edge_high, edge_low, hrev_ref, vpad_ref,
    band_ref, left_high, left_low, right_high, right_low, rows_ref, lane_ref, target_ref,
    difference_ref, likelihood_ref,
    template, border, kernels, sums,
):
    steps = own_ref.shape[0]
    half = own_ref.shape[2]
    columns = own_ref.shape[3]
    basis = hrev_ref.shape[0]
    taps = sums.shape[1]
    rim = taps // 2
    tile = tile_ref[0]
    wide = SHIFTS * GROUP
    place = (iota((GROUP, wide), 1) + wide - START) % wide % GROUP
    other_row = iota((GROUP, wide), 0) + 2 * rim - place
    valid = (other_row >= 0) & (other_row < GROUP) & (place <= 4 * rim)
    totals = []
    vectors = []
    stacks = []
    windows = []
    border[...] = jnp.zeros(border.shape, F32)
    template[...] = jnp.zeros(template.shape, F32)
    for step in range(steps):
        for index, ref in ((tile, own_ref), (1 - tile, other_ref)):
            first = pl.multiple_of(MARGIN + half * index, 16)
            template[step, pl.ds(first, half), :] = ref[step, 0]
        image = template[step, MARGIN : MARGIN + GROUP, :]
        mirrored = flip_rows(image)
        left = [[], []]
        for q in range(STRIDES):
            for side, piece in enumerate(split(shift_right(image, SHIFTS * q))):
                left[side].append(piece)
        left = [jnp.concatenate(pieces, axis=0) for pieces in left]
        right = [[], []]
        for s in range(SHIFTS):
            for side, piece in enumerate(split(shift_left(mirrored, s))):
                right[side].append(piece)
        right = [jnp.concatenate(pieces, axis=0) for pieces in right]
        auto = dot3(left, right, NT)
        ahead = dot3((left_high[step], left_low[step]), right, NT)
        near = [piece[: CROSS * GROUP] for piece in left]
        behind = dot3(near, (right_high[step], right_low[step]), NT)

        def align(block):
            turned = pltpu.roll(block, 0, 1, stride=1, stride_axis=0)
            return jnp.where(valid, turned, 0.0)

        weights = rows_ref[step]
        products = []
        for q in range(STRIDES):
            high, low = split(align(auto[q * GROUP : (q + 1) * GROUP]))
            gathered = dot(weights, jnp.concatenate([high, low], axis=0), NN)
            products.append(pltpu.roll(gathered, 0, 1, stride=1, stride_axis=0))
        partial = dot3(split(jnp.concatenate(products, axis=0)), (vb_high[...], vb_low[...]), NN)
        total = None
        for q in range(STRIDES):
            high, low = split(partial[q * TAP_PAD : (q + 1) * TAP_PAD])
            mixed = dot(vq_ref[...], jnp.concatenate([high, low, high], axis=0), NN)
            term = mixed * hc_ref[q]
            total = term if total is None else total + term
        total = total[:, :LANES] + total[:, LANES:]
        totals.append(total + pltpu.roll(total, GROUP, 1))

        vector = None
        for q in range(CROSS):
            here = slice(q * GROUP, (q + 1) * GROUP)
            for index, block in ((q, ahead), (CROSS + q, behind)):
                row = jnp.sum(align(block[here]), axis=0, keepdims=True)
                term = vh_ref[index] * row
                vector = term if vector is None else vector + term
        vectors.append(jnp.sum(vector, axis=1, keepdims=True))

        lane = iota((GROUP, LANES), 1)
        far = pltpu.roll(image[:, columns - LANES :], 2 * rim, 1)
        border[step, MARGIN : MARGIN + GROUP, :] = jnp.where(
            lane < rim, image[:, :LANES], jnp.where(lane < 2 * rim, far, 0.0)
        )
        chunks = []
        for t in range(4):
            chunk = None
            for g in range(EDGE_TAPS):
                tap = EDGE_TAPS * t + g
                if tap < taps:
                    piece = border[step, tap + MARGIN - rim : tap + MARGIN - rim + GROUP, :]
                    piece = pltpu.roll(piece, 2 * rim * g, 1) if g else piece
                    chunk = piece if chunk is None else chunk + piece
            chunks.append(chunk)
        stacks.append(jnp.concatenate(chunks, axis=1))

        top = MARGIN - rim
        low_top = MARGIN + half - 2 * rim
        windows.append(
            jnp.where(
                tile == 0,
                template[step, top : top + GROUP, :],
                template[step, low_top : low_top + GROUP, :],
            )
        )

    stack = split(jnp.concatenate(stacks, axis=0))
    outside = dot3((edge_high[...], edge_low[...]), stack, NT)
    outside = jnp.concatenate(
        [outside[e * basis : (e + 1) * basis] for e in range(2 * rim)], axis=1
    )
    out_high, out_low = split(outside)

    kept = []
    for step in range(steps):
        keep = jnp.concatenate([lane_ref[step]] * (2 * rim), axis=1)
        kept.append(split(outside * keep))
    all_high = jnp.concatenate([piece[0] for piece in kept], axis=0)
    all_low = jnp.concatenate([piece[1] for piece in kept], axis=0)
    removed_all = dot(all_high, out_high, NT) + (dot(all_high, out_low, NT) + dot(all_low, out_high, NT))

    row = iota((basis, LANES), 0)
    lane = iota((basis, LANES), 1)
    systems = []
    for step in range(steps):
        removed = removed_all[step * basis : (step + 1) * basis]
        square = jnp.concatenate(
            [totals[step], jnp.zeros((LANES - basis, LANES), F32)], axis=0
        )
        matrix = (square + square.T)[:basis]
        removed = jnp.concatenate([removed, jnp.zeros((basis, LANES - basis), F32)], axis=1)
        matrix = jnp.where(lane < basis, matrix - removed, 0.0)
        trace = jnp.sum(jnp.where(row == lane, matrix, 0.0), keepdims=True)
        system = jnp.where(row == lane, matrix + RIDGE * trace / basis, matrix)
        systems.append(jnp.where(lane == basis, vectors[step], system))
    coefficients = solve(systems)
    for step in range(steps):
        reverse = exact(coefficients[step] * vpad_ref[...], hrev_ref[...], TN)
        write_bands(reverse, taps, kernels.at[step])
    founds = []
    for step in range(steps):
        left = columns_for_bands(windows[step], rim)
        modelled = apply_bands(left, kernels.at[step], sums.at[step], GROUP, taps, half + rim)
        founds.append(target_ref[step] - modelled)
    for step in range(steps):
        found = founds[step]
        difference_ref[step, 0] = jnp.where(tile == 0, found[:half], found[rim:])
        tall = jnp.concatenate(
            [found, jnp.zeros((GROUP - half - rim, columns), F32)], axis=0
        )
        tall = jnp.where(tile == 0, pltpu.roll(tall, rim, 0), tall)
        left = columns_for_bands(tall, rim)
        likelihood_ref[step, 0] = apply_bands(
            left, band_ref, sums.at[step], GROUP, taps, half
        )


def in_vmem(count):
    return [pl.BlockSpec(memory_space=pltpu.VMEM)] * count


def in_smem(count):
    return [pl.BlockSpec(memory_space=pltpu.SMEM)] * count


def run_prepare(tile, vertical, horizontal, psf, own, other, mask, mask_other):
    basis, taps = vertical.shape
    steps, _, half, columns = own.shape
    wide = SHIFTS * GROUP
    shapes = [
        ((wide, wide), BF16), ((wide, wide), BF16),
        ((basis, 3 * TAP_PAD), BF16),
        ((STRIDES, basis, wide), F32),
        ((2 * CROSS, basis, wide), F32),
        ((2 * (taps // 2) * basis, 4 * LANES), BF16), ((2 * (taps // 2) * basis, 4 * LANES), BF16),
        ((basis, LANES), F32), ((basis, LANES), F32),
        ((4 * LANES, (taps + 1) * LANES), BF16),
        ((steps, CROSS * GROUP, columns), BF16), ((steps, CROSS * GROUP, columns), BF16),
        ((steps, wide, columns), BF16), ((steps, wide, columns), BF16),
        ((steps, TAP_PAD, 2 * GROUP), BF16),
        ((steps, 1, LANES), F32),
        ((steps, half + taps // 2, columns), F32),
    ]
    return pl.pallas_call(
        prepare,
        out_shape=[jax.ShapeDtypeStruct(shape, dtype) for shape, dtype in shapes],
        in_specs=in_smem(1) + in_vmem(7),
        out_specs=in_vmem(len(shapes)),
        scratch_shapes=[
            pltpu.VMEM((GROUP, TAP_PAD), F32),
            pltpu.VMEM((GROUP, TAP_PAD), F32),
            pltpu.VMEM((GROUP, LANES), F32),
            pltpu.VMEM((TAP_PAD, TAP_PAD), F32),
            pltpu.VMEM((GROUP, columns), F32),
            pltpu.VMEM((TAP_PAD, LANES), F32),
        ],
        compiler_params=pltpu.CompilerParams(vmem_limit_bytes=24 << 20),
        cost_estimate=pl.CostEstimate(flops=4_000_000_000, bytes_accessed=8_000_000, transcendentals=0),
        name="prepare",
    )(tile, vertical, horizontal, psf, own, other, mask, mask_other)


def run_fit(tile, own, other, prepared, taps):
    steps, _, half, columns = own.shape
    blocks = columns // LANES
    return pl.pallas_call(
        fit,
        out_shape=[jax.ShapeDtypeStruct(own.shape, F32)] * 2,
        in_specs=in_smem(1) + in_vmem(2 + len(prepared)),
        out_specs=in_vmem(2),
        scratch_shapes=[
            pltpu.VMEM((steps, GROUP + 2 * MARGIN, columns), F32),
            pltpu.VMEM((steps, GROUP + 2 * MARGIN, LANES), F32),
            pltpu.VMEM((steps, 4 * LANES, (taps + 1) * LANES), BF16),
            pltpu.VMEM((steps, taps, blocks * GROUP, LANES), F32),
        ],
        compiler_params=pltpu.CompilerParams(vmem_limit_bytes=32 << 20),
        cost_estimate=pl.CostEstimate(flops=20_000_000_000, bytes_accessed=16_000_000, transcendentals=0),
        name="fit",
    )(tile, own, other, *prepared)


def exchange(block, bit):
    count = lax.axis_size("visit")
    return lax.ppermute(block, "visit", [(i, i ^ bit) for i in range(count)])


def choose(block, arrived, distance, bit):
    count = lax.axis_size("visit")
    holds = jnp.bitwise_and(distance, count - bit) == 0
    return jnp.where(holds.reshape(-1, 1, 1, 1), block, arrived)


def on_device(templates, science, stamp_mask, owner, visit_map, vertical, horizontal, psf):
    swap = [(0, 1), (1, 0)]
    tile = lax.axis_index("tile").astype(jnp.int32).reshape(1)
    count = lax.axis_size("visit")
    block = templates
    arrived = exchange(block, 1) if count > 1 else block
    science_other = lax.ppermute(science, "tile", swap)
    mask_other = lax.ppermute(stamp_mask, "tile", swap)
    distance = jnp.bitwise_xor(visit_map[owner], lax.axis_index("visit"))
    arrived, distance, science_other, mask_other = lax.optimization_barrier(
        (arrived, distance, science_other, mask_other)
    )
    block = choose(block, arrived, distance, 1)
    arrived = exchange(block, 2) if count > 2 else block
    prepared = run_prepare(
        tile, vertical, horizontal, psf, science, science_other, stamp_mask, mask_other
    )
    arrived, prepared = lax.optimization_barrier((arrived, prepared))
    block = choose(block, arrived, distance, 2)
    bit = 4
    while bit < count:
        block = choose(block, exchange(block, bit), distance, bit)
        bit *= 2
    block_other = lax.ppermute(block, "tile", swap)
    return tuple(run_fit(tile, block, block_other, prepared, vertical.shape[1]))


def solution(mesh):
    placed = (
        P(None, ("groups", "visit"), "tile", None),
        P(None, ("groups", "visit"), "tile", None),
        P(None, ("groups", "visit"), "tile"),
        P("groups"),
        P("groups"),
        P(),
        P(),
        P(),
    )
    return jax.shard_map(
        on_device,
        mesh=mesh,
        in_specs=placed,
        out_specs=(
            P(None, ("groups", "visit"), "tile", None),
            P(None, ("groups", "visit"), "tile", None),
        ),
        check_vma=False,
    )
```

```python
import jax
import jax.numpy as jnp
from jax import lax
from jax.experimental import pallas as pl
from jax.experimental.pallas import tpu as pltpu
from jax.sharding import PartitionSpec as P

RIDGE = 0.05
F32 = jnp.float32
BF16 = jnp.bfloat16
HIGHEST = lax.Precision.HIGHEST
NN = (((1,), (0,)), ((), ()))
NT = (((1,), (1,)), ((), ()))
TN = (((0,), (0,)), ((), ()))

LANES = 128
GROUP = 64
SHIFTS = 4
STRIDES = 6
CROSS = 3
EDGE_TAPS = 6
TAP_PAD = 32
REST = 32
PANEL = 8
MARGIN = 16
START = 43


def iota(shape, dim):
    return lax.broadcasted_iota(jnp.int32, shape, dim)


def split(x):
    high = x.astype(BF16)
    return high, (x - high.astype(F32)).astype(BF16)


def dot(a, b, dims):
    return lax.dot_general(a, b, dims, preferred_element_type=F32)


def dot3(a, b, dims):
    return dot(a[0], b[0], dims) + (dot(a[0], b[1], dims) + dot(a[1], b[0], dims))


def exact(a, b, dims):
    return lax.dot_general(a, b, dims, precision=HIGHEST, preferred_element_type=F32)


def shift_right(x, amount):
    if amount == 0:
        return x
    return jnp.where(iota(x.shape, 1) >= amount, pltpu.roll(x, amount, 1), 0.0)


def shift_left(x, amount):
    if amount == 0:
        return x
    width = x.shape[1]
    return jnp.where(iota(x.shape, 1) < width - amount, pltpu.roll(x, width - amount, 1), 0.0)


def flip_rows(x):
    count = x.shape[0]
    mirror = (iota((count, count), 0) + iota((count, count), 1) == count - 1).astype(BF16)
    high, low = split(x)
    return dot(mirror, high, NN) + dot(mirror, low, NN)


def store_split(refs, index, x):
    high, low = split(x)
    refs[0][index] = high
    refs[1][index] = low


def write_bands(reverse, taps, ref):
    row = iota((LANES, LANES), 0)
    lane = iota((LANES, LANES), 1)
    ref[3 * LANES + 3 * REST :, :] = jnp.zeros((LANES - 3 * REST, ref.shape[1]), BF16)
    ref[:, taps * LANES :] = jnp.zeros((ref.shape[0], ref.shape[1] - taps * LANES), BF16)
    for tap in range(taps):
        base = jnp.broadcast_to(reverse[tap : tap + 1, :], (LANES, LANES))
        turned = pltpu.roll(base, 0, 1, stride=1, stride_axis=0)
        here = slice(tap * LANES, (tap + 1) * LANES)
        high, low = split(jnp.where(lane <= row, turned, 0.0))
        ref[0:LANES, here] = high
        ref[LANES : 2 * LANES, here] = high
        ref[2 * LANES : 3 * LANES, here] = low
        high, low = split(jnp.where(lane[:REST] > row[:REST], turned[:REST], 0.0))
        ref[3 * LANES : 3 * LANES + REST, here] = high
        ref[3 * LANES + REST : 3 * LANES + 2 * REST, here] = high
        ref[3 * LANES + 2 * REST : 3 * LANES + 3 * REST, here] = low


def prepare(
    tile_ref, vertical_ref, horizontal_ref, psf_ref, own_ref, other_ref, mask_ref, mask_other_ref,
    vb_high, vb_low, vq_ref, hc_ref, vh_ref, edge_high, edge_low, hrev_ref, vpad_ref,
    band_ref, left_high, left_low, right_high, right_low, rows_ref, lane_ref, target_ref,
    v_pad, h_pad, h_wide, psf_pad, science, chosen,
):
    basis, taps = vertical_ref.shape
    steps = own_ref.shape[0]
    rim = taps // 2
    half = own_ref.shape[2]
    tile = tile_ref[0]
    v_pad[...] = jnp.zeros(v_pad.shape, F32)
    h_pad[...] = jnp.zeros(h_pad.shape, F32)
    h_wide[...] = jnp.zeros(h_wide.shape, F32)
    psf_pad[...] = jnp.zeros(psf_pad.shape, F32)
    v_pad[:basis, :taps] = vertical_ref[...]
    h_pad[:basis, :taps] = horizontal_ref[...]
    h_wide[:basis, :taps] = horizontal_ref[...]
    psf_pad[:taps, :taps] = psf_ref[...]
    v_all = v_pad[...]
    v = v_all[:basis]
    h = h_pad[:basis]
    wide = SHIFTS * GROUP

    def pick(width, index):
        return (iota((TAP_PAD, width), 0) == index).astype(F32)

    lane = (iota((TAP_PAD, wide), 1) + wide - START) % wide
    turn, place = lane // GROUP, lane % GROUP

    def source(shape):
        return (iota(shape, 0) + wide - START - TAP_PAD + 1) % wide

    select = 2 * rim - source((wide, TAP_PAD)) % GROUP == iota((wide, TAP_PAD), 1)
    every = exact(select.astype(F32), jnp.concatenate([v_all] * SHIFTS, axis=0), NT)
    same = source((wide, wide)) // GROUP == iota((wide, wide), 1) // GROUP
    store_split((vb_high, vb_low), (slice(None), slice(None)), jnp.where(same, every, 0.0))

    mirror = iota((TAP_PAD, TAP_PAD), 0) + iota((TAP_PAD, TAP_PAD), 1) == TAP_PAD - 1
    v_high, v_low = split(exact(v, mirror.astype(F32), NN))
    vq_ref[:, 0:TAP_PAD] = v_high
    vq_ref[:, TAP_PAD : 2 * TAP_PAD] = v_high
    vq_ref[:, 2 * TAP_PAD : 3 * TAP_PAD] = v_low

    h_all = h_wide[...]
    for q in range(STRIDES):
        pieces = []
        for s in range(SHIFTS):
            distance = SHIFTS * q + s
            pieces.append(pltpu.roll(h_all, (LANES - distance) % LANES, 1))
        both = exact(h_all[:basis], jnp.concatenate(pieces, axis=0), NT)
        if q == 0:
            both = jnp.where(iota(both.shape, 1) < GROUP, 0.5 * both, both)
        hc_ref[q] = both

    down = exact(v, pick(wide, 3 * rim - place), NN)
    up = exact(v, pick(wide, place - rim), NN)
    for q in range(CROSS):
        ahead = exact(h, pick(wide, rim + SHIFTS * q + turn), NN)
        behind = exact(h, pick(wide, rim - SHIFTS * q - turn), NN)
        if q == 0:
            behind = jnp.where(turn[:1] == 0, 0.0, behind)
        vh_ref[q] = down * ahead
        vh_ref[CROSS + q] = up * behind

    narrow = iota((TAP_PAD, LANES), 1)
    part = narrow // (2 * rim)
    column = narrow % (2 * rim)
    used = part < EDGE_TAPS
    spread_v = jnp.concatenate(
        [
            exact(v, pick(LANES, jnp.where(used, EDGE_TAPS * t + part, -1)), NN)
            for t in range(4)
        ],
        axis=1,
    )
    for e in range(2 * rim):
        offset = 2 * rim - e if e < rim else -e
        spread_h = exact(h, pick(LANES, jnp.where(used, column + offset, -1)), NN)
        store_split(
            (edge_high, edge_low),
            (slice(e * basis, (e + 1) * basis), slice(None)),
            spread_v * jnp.concatenate([spread_h] * 4, axis=1),
        )

    back = pick(LANES, (LANES - narrow) % LANES)
    hrev_ref[...] = exact(h, back, NN)
    vpad_ref[...] = jnp.zeros(vpad_ref.shape, F32)
    vpad_ref[:, :TAP_PAD] = v
    write_bands(exact(psf_pad[...], back, NN), taps, band_ref)

    for step in range(steps):
        science[pl.ds(half * tile, half), :] = own_ref[step, 0]
        science[pl.ds(half * (1 - tile), half), :] = other_ref[step, 0]
        first = jnp.where(tile == 0, mask_ref[step], mask_other_ref[step]).astype(F32)
        second = jnp.where(tile == 0, mask_other_ref[step], mask_ref[step]).astype(F32)
        mask = jnp.concatenate([first, second], axis=1)
        diagonal = iota((GROUP, GROUP), 0) == iota((GROUP, GROUP), 1)
        column_mask = jnp.sum(jnp.where(diagonal, mask, 0.0), axis=1, keepdims=True)
        masked = science[...] * column_mask
        mirrored = flip_rows(masked)
        for q in range(CROSS):
            store_split(
                (left_high, left_low),
                (step, slice(q * GROUP, (q + 1) * GROUP), slice(None)),
                shift_right(masked, SHIFTS * q),
            )
        for s in range(SHIFTS):
            store_split(
                (right_high, right_low),
                (step, slice(s * GROUP, (s + 1) * GROUP), slice(None)),
                shift_left(mirrored, s),
            )
        chosen[...] = jnp.zeros(chosen.shape, F32)
        single = jnp.concatenate([mask, jnp.zeros((1, GROUP), F32)], axis=1)
        for tap in range(taps):
            place_row = TAP_PAD - 1 - tap
            chosen[place_row : place_row + 1, :] = pltpu.roll(single, (tap - rim) % LANES, 1)
        moved = chosen[...][:, :GROUP]
        rows_ref[step] = jnp.concatenate([moved, moved], axis=1).astype(BF16)
        zero = jnp.zeros((1, GROUP), F32)
        ordered = [zero] * steps
        ordered[step] = mask
        lane_ref[step] = jnp.concatenate(ordered, axis=1)
        target_ref[step] = jnp.where(
            tile == 0, science[0 : half + rim, :], science[half - rim : 2 * half, :]
        )


def solve(systems):
    count, width = systems[0].shape
    row = iota((count, width), 0)
    lane = iota((count, width), 1)
    for first in range(0, count, PANEL):
        panels = [
            [
                jnp.broadcast_to(system[:, first + j : first + j + 1], (count, width))
                for j in range(PANEL)
            ]
            for system in systems
        ]
        for j in range(PANEL):
            pivot = first + j
            for index, panel in enumerate(panels):
                column = panel[j]
                factor = column * (1.0 / column[pivot : pivot + 1, :])
                factor = jnp.where(row == pivot, 0.0, factor)
                for m in range(j + 1, PANEL):
                    panel[m] = panel[m] - factor * panel[m][pivot : pivot + 1, :]
                system = systems[index]
                systems[index] = system - factor * system[pivot : pivot + 1, :]
    results = []
    for system in systems:
        scale = jnp.sum(jnp.where(row == lane, system, 0.0), axis=1, keepdims=True)
        results.append(system[:, count : count + 1] / scale)
    return results


def columns_for_bands(image, rim):
    rows, columns = image.shape
    padded = pltpu.roll(
        jnp.concatenate([image, jnp.zeros((rows, LANES), F32)], axis=1), rim, 1
    )
    high, low = split(padded)
    lane = iota((rows, LANES), 1)
    blocks = []
    for c in range(columns // LANES):
        here = slice(c * LANES, (c + 1) * LANES)
        there = slice((c + 1) * LANES, (c + 2) * LANES)
        next_high = high[:, there].astype(F32)
        next_low = low[:, there].astype(F32)
        rest = jnp.where(
            lane < REST,
            next_high,
            jnp.where(
                lane < 2 * REST,
                pltpu.roll(next_low, REST, 1),
                jnp.where(lane < 3 * REST, pltpu.roll(next_high, 2 * REST, 1), 0.0),
            ),
        )
        blocks.append(
            jnp.concatenate([high[:, here], low[:, here], high[:, here], rest.astype(BF16)], axis=1)
        )
    return jnp.concatenate(blocks, axis=0)


def apply_bands(left, band_ref, sums, rows, taps, out_rows):
    block_count = left.shape[0] // rows
    for tap in range(0, taps, 2):
        count = min(2, taps - tap)
        both = dot(left, band_ref[:, tap * LANES : (tap + count) * LANES], NN)
        for side in range(count):
            sums[tap + side] = both[:, side * LANES : (side + 1) * LANES]
    blocks = []
    for c in range(block_count):
        total = None
        for tap in range(taps):
            first = c * rows + tap
            term = sums[tap, first : first + out_rows, :]
            total = term if total is None else total + term
        blocks.append(total)
    return jnp.concatenate(blocks, axis=1)


def fit(
    tile_ref, own_ref, other_ref,
    vb_high, vb_low, vq_ref, hc_ref, vh_ref, edge_high, edge_low, hrev_ref, vpad_ref,
    band_ref, left_high, left_low, right_high, right_low, rows_ref, lane_ref, target_ref,
    difference_ref, likelihood_ref,
    template, border, kernels, sums, spread_window, difference, likelihood, sems,
):
    steps = own_ref.shape[0]
    half = own_ref.shape[2]
    columns = own_ref.shape[3]
    basis = hrev_ref.shape[0]
    taps = sums.shape[1]
    rim = taps // 2
    tile = tile_ref[0]
    wide = SHIFTS * GROUP
    place = (iota((GROUP, wide), 1) + wide - START) % wide % GROUP
    other_row = iota((GROUP, wide), 0) + 2 * rim - place
    valid = (other_row >= 0) & (other_row < GROUP) & (place <= 4 * rim)
    every = range(steps)
    border[...] = jnp.zeros(border.shape, F32)
    template[...] = jnp.zeros(template.shape, F32)
    images = []
    for step in every:
        for index, ref in ((tile, own_ref), (1 - tile, other_ref)):
            first = pl.multiple_of(MARGIN + half * index, 16)
            template[step, pl.ds(first, half), :] = ref[step, 0]
        images.append(template[step, MARGIN : MARGIN + GROUP, :])
    mirrored = [flip_rows(image) for image in images]
    lefts = []
    for image in images:
        pieces = [split(shift_right(image, SHIFTS * q)) for q in range(STRIDES)]
        lefts.append([jnp.concatenate([piece[i] for piece in pieces], axis=0) for i in (0, 1)])
    rights = []
    for image in mirrored:
        pieces = [split(shift_left(image, s)) for s in range(SHIFTS)]
        rights.append([jnp.concatenate([piece[i] for piece in pieces], axis=0) for i in (0, 1)])

    stacks = []
    lane = iota((GROUP, LANES), 1)
    for step, image in enumerate(images):
        far = pltpu.roll(image[:, columns - LANES :], 2 * rim, 1)
        border[step, MARGIN : MARGIN + GROUP, :] = jnp.where(
            lane < rim, image[:, :LANES], jnp.where(lane < 2 * rim, far, 0.0)
        )
        chunks = []
        for t in range(4):
            chunk = None
            for g in range(EDGE_TAPS):
                tap = EDGE_TAPS * t + g
                if tap < taps:
                    piece = border[step, tap + MARGIN - rim : tap + MARGIN - rim + GROUP, :]
                    piece = pltpu.roll(piece, 2 * rim * g, 1) if g else piece
                    chunk = piece if chunk is None else chunk + piece
            chunks.append(chunk)
        stacks.append(jnp.concatenate(chunks, axis=1))

    autos = [dot3(lefts[step], rights[step], NT) for step in every]
    aheads = [dot3((left_high[step], left_low[step]), rights[step], NT) for step in every]
    behinds = []
    for step in every:
        near = [piece[: CROSS * GROUP] for piece in lefts[step]]
        behinds.append(dot3(near, (right_high[step], right_low[step]), NT))

    def align(block):
        turned = pltpu.roll(block, 0, 1, stride=1, stride_axis=0)
        return jnp.where(valid, turned, 0.0)

    aligned = []
    for step in every:
        parts = [split(align(autos[step][q * GROUP : (q + 1) * GROUP])) for q in range(STRIDES)]
        aligned.append([jnp.concatenate(part, axis=0) for part in parts])
    products = []
    for step in every:
        gathered = [dot(rows_ref[step], part, NN) for part in aligned[step]]
        turned = [pltpu.roll(part, 0, 1, stride=1, stride_axis=0) for part in gathered]
        products.append(split(jnp.concatenate(turned, axis=0)))
    stack = split(jnp.concatenate(stacks, axis=0))
    outside = dot3((edge_high[...], edge_low[...]), stack, NT)
    partials = [dot3(products[step], (vb_high[...], vb_low[...]), NN) for step in every]
    outside = jnp.concatenate(
        [outside[e * basis : (e + 1) * basis] for e in range(2 * rim)], axis=1
    )
    out_high, out_low = split(outside)
    totals = []
    for step in every:
        total = None
        for q in range(STRIDES):
            high, low = split(partials[step][q * TAP_PAD : (q + 1) * TAP_PAD])
            mixed = dot(vq_ref[...], jnp.concatenate([high, low, high], axis=0), NN)
            term = mixed * hc_ref[q]
            total = term if total is None else total + term
        total = total[:, :LANES] + total[:, LANES:]
        totals.append(total + pltpu.roll(total, GROUP, 1))
    vectors = []
    for step in every:
        vector = None
        for q in range(CROSS):
            here = slice(q * GROUP, (q + 1) * GROUP)
            for index, block in ((q, aheads[step]), (CROSS + q, behinds[step])):
                line = jnp.sum(align(block[here]), axis=0, keepdims=True)
                term = vh_ref[index] * line
                vector = term if vector is None else vector + term
        vectors.append(jnp.sum(vector, axis=1, keepdims=True))

    kept = []
    for step in range(steps):
        keep = jnp.concatenate([lane_ref[step]] * (2 * rim), axis=1)
        kept.append(split(outside * keep))
    all_high = jnp.concatenate([piece[0] for piece in kept], axis=0)
    all_low = jnp.concatenate([piece[1] for piece in kept], axis=0)
    removed_all = dot(all_high, out_high, NT) + (dot(all_high, out_low, NT) + dot(all_low, out_high, NT))

    row = iota((basis, LANES), 0)
    lane = iota((basis, LANES), 1)
    systems = []
    for step in range(steps):
        removed = removed_all[step * basis : (step + 1) * basis]
        square = jnp.concatenate(
            [totals[step], jnp.zeros((LANES - basis, LANES), F32)], axis=0
        )
        matrix = (square + square.T)[:basis]
        removed = jnp.concatenate([removed, jnp.zeros((basis, LANES - basis), F32)], axis=1)
        matrix = jnp.where(lane < basis, matrix - removed, 0.0)
        trace = jnp.sum(jnp.where(row == lane, matrix, 0.0), keepdims=True)
        system = jnp.where(row == lane, matrix + RIDGE * trace / basis, matrix)
        systems.append(jnp.where(lane == basis, vectors[step], system))
    top = MARGIN - rim
    low_top = MARGIN + half - 2 * rim
    for step in every:
        window = jnp.where(
            tile == 0,
            template[step, top : top + GROUP, :],
            template[step, low_top : low_top + GROUP, :],
        )
        spread_window[step] = columns_for_bands(window, rim)
    coefficients = solve(systems)
    for step in every:
        reverse = exact(coefficients[step] * vpad_ref[...], hrev_ref[...], TN)
        write_bands(reverse, taps, kernels.at[step])
    founds = []
    copies = []
    for step in every:
        modelled = apply_bands(
            spread_window[step], kernels.at[step], sums.at[step], GROUP, taps, half + rim
        )
        founds.append(target_ref[step] - modelled)
        difference[step, 0] = jnp.where(tile == 0, founds[step][:half], founds[step][rim:])
        copies.append(
            pltpu.make_async_copy(difference.at[step], difference_ref.at[step], sems.at[0, step])
        )
        copies[-1].start()
    for step in every:
        tall = jnp.concatenate(
            [founds[step], jnp.zeros((GROUP - half - rim, columns), F32)], axis=0
        )
        tall = jnp.where(tile == 0, pltpu.roll(tall, rim, 0), tall)
        likelihood[step, 0] = apply_bands(
            columns_for_bands(tall, rim), band_ref, sums.at[step], GROUP, taps, half
        )
        copies.append(
            pltpu.make_async_copy(likelihood.at[step], likelihood_ref.at[step], sems.at[1, step])
        )
        copies[-1].start()
    for copy in copies:
        copy.wait()


def in_vmem(count):
    return [pl.BlockSpec(memory_space=pltpu.VMEM)] * count


def in_smem(count):
    return [pl.BlockSpec(memory_space=pltpu.SMEM)] * count


def run_prepare(tile, vertical, horizontal, psf, own, other, mask, mask_other):
    basis, taps = vertical.shape
    steps, _, half, columns = own.shape
    wide = SHIFTS * GROUP
    shapes = [
        ((wide, wide), BF16), ((wide, wide), BF16),
        ((basis, 3 * TAP_PAD), BF16),
        ((STRIDES, basis, wide), F32),
        ((2 * CROSS, basis, wide), F32),
        ((2 * (taps // 2) * basis, 4 * LANES), BF16), ((2 * (taps // 2) * basis, 4 * LANES), BF16),
        ((basis, LANES), F32), ((basis, LANES), F32),
        ((4 * LANES, (taps + 1) * LANES), BF16),
        ((steps, CROSS * GROUP, columns), BF16), ((steps, CROSS * GROUP, columns), BF16),
        ((steps, wide, columns), BF16), ((steps, wide, columns), BF16),
        ((steps, TAP_PAD, 2 * GROUP), BF16),
        ((steps, 1, LANES), F32),
        ((steps, half + taps // 2, columns), F32),
    ]
    return pl.pallas_call(
        prepare,
        out_shape=[jax.ShapeDtypeStruct(shape, dtype) for shape, dtype in shapes],
        in_specs=in_smem(1) + in_vmem(7),
        out_specs=in_vmem(len(shapes)),
        scratch_shapes=[
            pltpu.VMEM((GROUP, TAP_PAD), F32),
            pltpu.VMEM((GROUP, TAP_PAD), F32),
            pltpu.VMEM((GROUP, LANES), F32),
            pltpu.VMEM((TAP_PAD, TAP_PAD), F32),
            pltpu.VMEM((GROUP, columns), F32),
            pltpu.VMEM((TAP_PAD, LANES), F32),
        ],
        compiler_params=pltpu.CompilerParams(vmem_limit_bytes=24 << 20),
        cost_estimate=pl.CostEstimate(flops=4_000_000_000, bytes_accessed=8_000_000, transcendentals=0),
        name="prepare",
    )(tile, vertical, horizontal, psf, own, other, mask, mask_other)


def run_fit(tile, own, other, prepared, taps):
    steps, _, half, columns = own.shape
    blocks = columns // LANES
    return pl.pallas_call(
        fit,
        out_shape=[jax.ShapeDtypeStruct(own.shape, F32)] * 2,
        in_specs=in_smem(1) + in_vmem(2 + len(prepared)),
        out_specs=[pl.BlockSpec(memory_space=pl.ANY)] * 2,
        scratch_shapes=[
            pltpu.VMEM((steps, GROUP + 2 * MARGIN, columns), F32),
            pltpu.VMEM((steps, GROUP + 2 * MARGIN, LANES), F32),
            pltpu.VMEM((steps, 4 * LANES, (taps + 1) * LANES), BF16),
            pltpu.VMEM((steps, taps, blocks * GROUP, LANES), F32),
            pltpu.VMEM((steps, blocks * GROUP, 4 * LANES), BF16),
            pltpu.VMEM((steps, 1, half, columns), F32),
            pltpu.VMEM((steps, 1, half, columns), F32),
            pltpu.SemaphoreType.DMA((2, steps)),
        ],
        compiler_params=pltpu.CompilerParams(vmem_limit_bytes=32 << 20),
        cost_estimate=pl.CostEstimate(flops=20_000_000_000, bytes_accessed=16_000_000, transcendentals=0),
        name="fit",
    )(tile, own, other, *prepared)


def exchange(block, bit):
    count = lax.axis_size("visit")
    return lax.ppermute(block, "visit", [(i, i ^ bit) for i in range(count)])


def choose(block, arrived, distance, bit):
    count = lax.axis_size("visit")
    holds = jnp.bitwise_and(distance, count - bit) == 0
    return jnp.where(holds.reshape(-1, 1, 1, 1), block, arrived)


def on_device(templates, science, stamp_mask, owner, visit_map, vertical, horizontal, psf):
    swap = [(0, 1), (1, 0)]
    tile = lax.axis_index("tile").astype(jnp.int32).reshape(1)
    count = lax.axis_size("visit")
    block = templates
    arrived = exchange(block, 1) if count > 1 else block
    science_other = lax.ppermute(science, "tile", swap)
    mask_other = lax.ppermute(stamp_mask, "tile", swap)
    distance = jnp.bitwise_xor(visit_map[owner], lax.axis_index("visit"))
    arrived, distance, science_other, mask_other = lax.optimization_barrier(
        (arrived, distance, science_other, mask_other)
    )
    block = choose(block, arrived, distance, 1)
    bit = 2
    prepared = None
    while bit < count:
        arrived = exchange(block, bit)
        bit *= 2
        if bit >= count:
            prepared = run_prepare(
                tile, vertical, horizontal, psf, science, science_other, stamp_mask, mask_other
            )
            arrived, prepared = lax.optimization_barrier((arrived, prepared))
        block = choose(block, arrived, distance, bit // 2)
    block_other = lax.ppermute(block, "tile", swap)
    return tuple(run_fit(tile, block, block_other, prepared, vertical.shape[1]))


def solution(mesh):
    placed = (
        P(None, ("groups", "visit"), "tile", None),
        P(None, ("groups", "visit"), "tile", None),
        P(None, ("groups", "visit"), "tile"),
        P("groups"),
        P("groups"),
        P(),
        P(),
        P(),
    )
    return jax.shard_map(
        on_device,
        mesh=mesh,
        in_specs=placed,
        out_specs=(
            P(None, ("groups", "visit"), "tile", None),
            P(None, ("groups", "visit"), "tile", None),
        ),
        check_vma=False,
    )
```

```python
import jax
import jax.numpy as jnp
from jax import lax
from jax.experimental import pallas as pl
from jax.experimental.pallas import tpu as pltpu
from jax.sharding import PartitionSpec as P

RIDGE = 0.05
F32 = jnp.float32
BF16 = jnp.bfloat16
HIGHEST = lax.Precision.HIGHEST
NN = (((1,), (0,)), ((), ()))
NT = (((1,), (1,)), ((), ()))
TN = (((0,), (0,)), ((), ()))

LANES = 128
GROUP = 64
SHIFTS = 4
STRIDES = 6
CROSS = 3
EDGE_TAPS = 6
TAP_PAD = 32
REST = 32
PANEL = 8
MARGIN = 16
START = 43


def iota(shape, dim):
    return lax.broadcasted_iota(jnp.int32, shape, dim)


def split(x):
    high = x.astype(BF16)
    return high, (x - high.astype(F32)).astype(BF16)


def dot(a, b, dims):
    return lax.dot_general(a, b, dims, preferred_element_type=F32)


def dot3(a, b, dims):
    return dot(a[0], b[0], dims) + (dot(a[0], b[1], dims) + dot(a[1], b[0], dims))


def exact(a, b, dims):
    return lax.dot_general(a, b, dims, precision=HIGHEST, preferred_element_type=F32)


def shift_right(x, amount):
    if amount == 0:
        return x
    return jnp.where(iota(x.shape, 1) >= amount, pltpu.roll(x, amount, 1), 0.0)


def shift_left(x, amount):
    if amount == 0:
        return x
    width = x.shape[1]
    return jnp.where(iota(x.shape, 1) < width - amount, pltpu.roll(x, width - amount, 1), 0.0)


def flip_rows(x):
    count = x.shape[0]
    mirror = (iota((count, count), 0) + iota((count, count), 1) == count - 1).astype(BF16)
    high, low = split(x)
    return dot(mirror, high, NN) + dot(mirror, low, NN)


def store_split(refs, index, x):
    high, low = split(x)
    refs[0][index] = high
    refs[1][index] = low


def write_bands(reverse, taps, ref):
    row = iota((LANES, LANES), 0)
    lane = iota((LANES, LANES), 1)
    ref[3 * LANES + 3 * REST :, :] = jnp.zeros((LANES - 3 * REST, ref.shape[1]), BF16)
    ref[:, taps * LANES :] = jnp.zeros((ref.shape[0], ref.shape[1] - taps * LANES), BF16)
    for tap in range(taps):
        base = jnp.broadcast_to(reverse[tap : tap + 1, :], (LANES, LANES))
        turned = pltpu.roll(base, 0, 1, stride=1, stride_axis=0)
        here = slice(tap * LANES, (tap + 1) * LANES)
        high, low = split(jnp.where(lane <= row, turned, 0.0))
        ref[0:LANES, here] = high
        ref[LANES : 2 * LANES, here] = high
        ref[2 * LANES : 3 * LANES, here] = low
        high, low = split(jnp.where(lane[:REST] > row[:REST], turned[:REST], 0.0))
        ref[3 * LANES : 3 * LANES + REST, here] = high
        ref[3 * LANES + REST : 3 * LANES + 2 * REST, here] = high
        ref[3 * LANES + 2 * REST : 3 * LANES + 3 * REST, here] = low


def prepare(
    tile_ref, vertical_ref, horizontal_ref, psf_ref, own_ref, other_ref, mask_ref, mask_other_ref,
    vb_high, vb_low, vq_ref, hc_ref, vh_ref, edge_high, edge_low, hrev_ref, vpad_ref,
    band_ref, left_high, left_low, right_high, right_low, rows_ref, lane_ref, target_ref,
    v_turned, h_turned, psf_pad, science, chosen,
):
    taps, basis = vertical_ref.shape
    steps = own_ref.shape[0]
    rim = taps // 2
    half = own_ref.shape[2]
    tile = tile_ref[0]
    v_turned[...] = jnp.zeros(v_turned.shape, F32)
    h_turned[...] = jnp.zeros(h_turned.shape, F32)
    psf_pad[...] = jnp.zeros(psf_pad.shape, F32)
    v_turned[:taps, :basis] = vertical_ref[...]
    h_turned[:taps, :basis] = horizontal_ref[...]
    psf_pad[:taps, :taps] = psf_ref[...]
    v_all = v_turned[...].T[:GROUP, :TAP_PAD]
    h_all = h_turned[...].T[:GROUP]
    v = v_all[:basis]
    h = h_all[:basis, :TAP_PAD]
    wide = SHIFTS * GROUP

    def pick(width, index):
        return (iota((TAP_PAD, width), 0) == index).astype(F32)

    lane = (iota((TAP_PAD, wide), 1) + wide - START) % wide
    turn, place = lane // GROUP, lane % GROUP

    def source(shape):
        return (iota(shape, 0) + wide - START - TAP_PAD + 1) % wide

    select = 2 * rim - source((wide, TAP_PAD)) % GROUP == iota((wide, TAP_PAD), 1)
    every = exact(select.astype(F32), jnp.concatenate([v_all] * SHIFTS, axis=0), NT)
    same = source((wide, wide)) // GROUP == iota((wide, wide), 1) // GROUP
    store_split((vb_high, vb_low), (slice(None), slice(None)), jnp.where(same, every, 0.0))

    mirror = iota((TAP_PAD, TAP_PAD), 0) + iota((TAP_PAD, TAP_PAD), 1) == TAP_PAD - 1
    v_high, v_low = split(exact(v, mirror.astype(F32), NN))
    vq_ref[:, 0:TAP_PAD] = v_high
    vq_ref[:, TAP_PAD : 2 * TAP_PAD] = v_high
    vq_ref[:, 2 * TAP_PAD : 3 * TAP_PAD] = v_low

    for q in range(STRIDES):
        pieces = []
        for s in range(SHIFTS):
            distance = SHIFTS * q + s
            pieces.append(pltpu.roll(h_all, (LANES - distance) % LANES, 1))
        both = exact(h_all[:basis], jnp.concatenate(pieces, axis=0), NT)
        if q == 0:
            both = jnp.where(iota(both.shape, 1) < GROUP, 0.5 * both, both)
        hc_ref[q] = both

    down = exact(v, pick(wide, 3 * rim - place), NN)
    up = exact(v, pick(wide, place - rim), NN)
    for q in range(CROSS):
        ahead = exact(h, pick(wide, rim + SHIFTS * q + turn), NN)
        behind = exact(h, pick(wide, rim - SHIFTS * q - turn), NN)
        if q == 0:
            behind = jnp.where(turn[:1] == 0, 0.0, behind)
        vh_ref[q] = down * ahead
        vh_ref[CROSS + q] = up * behind

    narrow = iota((TAP_PAD, LANES), 1)
    part = narrow // (2 * rim)
    column = narrow % (2 * rim)
    used = part < EDGE_TAPS
    spread_v = jnp.concatenate(
        [
            exact(v, pick(LANES, jnp.where(used, EDGE_TAPS * t + part, -1)), NN)
            for t in range(4)
        ],
        axis=1,
    )
    for e in range(2 * rim):
        offset = 2 * rim - e if e < rim else -e
        spread_h = exact(h, pick(LANES, jnp.where(used, column + offset, -1)), NN)
        store_split(
            (edge_high, edge_low),
            (slice(e * basis, (e + 1) * basis), slice(None)),
            spread_v * jnp.concatenate([spread_h] * 4, axis=1),
        )

    back = pick(LANES, (LANES - narrow) % LANES)
    hrev_ref[...] = exact(h, back, NN)
    vpad_ref[...] = jnp.zeros(vpad_ref.shape, F32)
    vpad_ref[:, :TAP_PAD] = v
    write_bands(exact(psf_pad[...], back, NN), taps, band_ref)

    for step in range(steps):
        science[pl.ds(half * tile, half), :] = own_ref[step, 0]
        science[pl.ds(half * (1 - tile), half), :] = other_ref[step, 0]
        first = jnp.where(tile == 0, mask_ref[step], mask_other_ref[step]).astype(F32)
        second = jnp.where(tile == 0, mask_other_ref[step], mask_ref[step]).astype(F32)
        mask = jnp.concatenate([first, second], axis=1)
        diagonal = iota((GROUP, GROUP), 0) == iota((GROUP, GROUP), 1)
        column_mask = jnp.sum(jnp.where(diagonal, mask, 0.0), axis=1, keepdims=True)
        masked = science[...] * column_mask
        mirrored = flip_rows(masked)
        for q in range(CROSS):
            store_split(
                (left_high, left_low),
                (step, slice(q * GROUP, (q + 1) * GROUP), slice(None)),
                shift_right(masked, SHIFTS * q),
            )
        for s in range(SHIFTS):
            store_split(
                (right_high, right_low),
                (step, slice(s * GROUP, (s + 1) * GROUP), slice(None)),
                shift_left(mirrored, s),
            )
        chosen[...] = jnp.zeros(chosen.shape, F32)
        single = jnp.concatenate([mask, jnp.zeros((1, GROUP), F32)], axis=1)
        for tap in range(taps):
            place_row = TAP_PAD - 1 - tap
            chosen[place_row : place_row + 1, :] = pltpu.roll(single, (tap - rim) % LANES, 1)
        moved = chosen[...][:, :GROUP]
        rows_ref[step] = jnp.concatenate([moved, moved], axis=1).astype(BF16)
        zero = jnp.zeros((1, GROUP), F32)
        ordered = [zero] * steps
        ordered[step] = mask
        lane_ref[step] = jnp.concatenate(ordered, axis=1)
        target_ref[step] = jnp.where(
            tile == 0, science[0 : half + rim, :], science[half - rim : 2 * half, :]
        )


def solve(systems):
    count, width = systems[0].shape
    row = iota((count, width), 0)
    lane = iota((count, width), 1)
    for first in range(0, count, PANEL):
        panels = [
            [
                jnp.broadcast_to(system[:, first + j : first + j + 1], (count, width))
                for j in range(PANEL)
            ]
            for system in systems
        ]
        for j in range(PANEL):
            pivot = first + j
            for index, panel in enumerate(panels):
                column = panel[j]
                factor = column * (1.0 / column[pivot : pivot + 1, :])
                factor = jnp.where(row == pivot, 0.0, factor)
                for m in range(j + 1, PANEL):
                    panel[m] = panel[m] - factor * panel[m][pivot : pivot + 1, :]
                system = systems[index]
                systems[index] = system - factor * system[pivot : pivot + 1, :]
    results = []
    for system in systems:
        scale = jnp.sum(jnp.where(row == lane, system, 0.0), axis=1, keepdims=True)
        results.append(system[:, count : count + 1] / scale)
    return results


def columns_for_bands(image, rim):
    rows, columns = image.shape
    padded = pltpu.roll(
        jnp.concatenate([image, jnp.zeros((rows, LANES), F32)], axis=1), rim, 1
    )
    high, low = split(padded)
    lane = iota((rows, LANES), 1)
    blocks = []
    for c in range(columns // LANES):
        here = slice(c * LANES, (c + 1) * LANES)
        there = slice((c + 1) * LANES, (c + 2) * LANES)
        next_high = high[:, there].astype(F32)
        next_low = low[:, there].astype(F32)
        rest = jnp.where(
            lane < REST,
            next_high,
            jnp.where(
                lane < 2 * REST,
                pltpu.roll(next_low, REST, 1),
                jnp.where(lane < 3 * REST, pltpu.roll(next_high, 2 * REST, 1), 0.0),
            ),
        )
        blocks.append(
            jnp.concatenate([high[:, here], low[:, here], high[:, here], rest.astype(BF16)], axis=1)
        )
    return jnp.concatenate(blocks, axis=0)


def apply_bands(left, band_ref, sums, rows, taps, out_rows):
    block_count = left.shape[0] // rows
    for tap in range(0, taps, 2):
        count = min(2, taps - tap)
        both = dot(left, band_ref[:, tap * LANES : (tap + count) * LANES], NN)
        for side in range(count):
            sums[tap + side] = both[:, side * LANES : (side + 1) * LANES]
    blocks = []
    for c in range(block_count):
        total = None
        for tap in range(taps):
            first = c * rows + tap
            term = sums[tap, first : first + out_rows, :]
            total = term if total is None else total + term
        blocks.append(total)
    return jnp.concatenate(blocks, axis=1)


def fit(
    tile_ref, own_ref, other_ref,
    vb_high, vb_low, vq_ref, hc_ref, vh_ref, edge_high, edge_low, hrev_ref, vpad_ref,
    band_ref, left_high, left_low, right_high, right_low, rows_ref, lane_ref, target_ref,
    difference_ref, likelihood_ref,
    template, border, kernels, sums, spread_window, difference, likelihood, sems,
):
    steps = own_ref.shape[0]
    half = own_ref.shape[2]
    columns = own_ref.shape[3]
    basis = hrev_ref.shape[0]
    taps = sums.shape[1]
    rim = taps // 2
    tile = tile_ref[0]
    wide = SHIFTS * GROUP
    place = (iota((GROUP, wide), 1) + wide - START) % wide % GROUP
    other_row = iota((GROUP, wide), 0) + 2 * rim - place
    valid = (other_row >= 0) & (other_row < GROUP) & (place <= 4 * rim)
    every = range(steps)
    border[...] = jnp.zeros(border.shape, F32)
    template[...] = jnp.zeros(template.shape, F32)
    images = []
    for step in every:
        for index, ref in ((tile, own_ref), (1 - tile, other_ref)):
            first = pl.multiple_of(MARGIN + half * index, 16)
            template[step, pl.ds(first, half), :] = ref[step, 0]
        images.append(template[step, MARGIN : MARGIN + GROUP, :])
    mirrored = [flip_rows(image) for image in images]
    lefts = []
    for image in images:
        pieces = [split(shift_right(image, SHIFTS * q)) for q in range(STRIDES)]
        lefts.append([jnp.concatenate([piece[i] for piece in pieces], axis=0) for i in (0, 1)])
    rights = []
    for image in mirrored:
        pieces = [split(shift_left(image, s)) for s in range(SHIFTS)]
        rights.append([jnp.concatenate([piece[i] for piece in pieces], axis=0) for i in (0, 1)])

    stacks = []
    lane = iota((GROUP, LANES), 1)
    for step, image in enumerate(images):
        far = pltpu.roll(image[:, columns - LANES :], 2 * rim, 1)
        border[step, MARGIN : MARGIN + GROUP, :] = jnp.where(
            lane < rim, image[:, :LANES], jnp.where(lane < 2 * rim, far, 0.0)
        )
        chunks = []
        for t in range(4):
            chunk = None
            for g in range(EDGE_TAPS):
                tap = EDGE_TAPS * t + g
                if tap < taps:
                    piece = border[step, tap + MARGIN - rim : tap + MARGIN - rim + GROUP, :]
                    piece = pltpu.roll(piece, 2 * rim * g, 1) if g else piece
                    chunk = piece if chunk is None else chunk + piece
            chunks.append(chunk)
        stacks.append(jnp.concatenate(chunks, axis=1))

    autos = [dot3(lefts[step], rights[step], NT) for step in every]
    aheads = [dot3((left_high[step], left_low[step]), rights[step], NT) for step in every]
    behinds = []
    for step in every:
        near = [piece[: CROSS * GROUP] for piece in lefts[step]]
        behinds.append(dot3(near, (right_high[step], right_low[step]), NT))

    def align(block):
        turned = pltpu.roll(block, 0, 1, stride=1, stride_axis=0)
        return jnp.where(valid, turned, 0.0)

    aligned = []
    for step in every:
        parts = [split(align(autos[step][q * GROUP : (q + 1) * GROUP])) for q in range(STRIDES)]
        aligned.append([jnp.concatenate(part, axis=0) for part in parts])
    products = []
    for step in every:
        gathered = [dot(rows_ref[step], part, NN) for part in aligned[step]]
        turned = [pltpu.roll(part, 0, 1, stride=1, stride_axis=0) for part in gathered]
        products.append(split(jnp.concatenate(turned, axis=0)))
    stack = split(jnp.concatenate(stacks, axis=0))
    outside = dot3((edge_high[...], edge_low[...]), stack, NT)
    partials = [dot3(products[step], (vb_high[...], vb_low[...]), NN) for step in every]
    outside = jnp.concatenate(
        [outside[e * basis : (e + 1) * basis] for e in range(2 * rim)], axis=1
    )
    out_high, out_low = split(outside)
    totals = []
    for step in every:
        total = None
        for q in range(STRIDES):
            high, low = split(partials[step][q * TAP_PAD : (q + 1) * TAP_PAD])
            mixed = dot(vq_ref[...], jnp.concatenate([high, low, high], axis=0), NN)
            term = mixed * hc_ref[q]
            total = term if total is None else total + term
        total = total[:, :LANES] + total[:, LANES:]
        totals.append(total + pltpu.roll(total, GROUP, 1))
    vectors = []
    for step in every:
        vector = None
        for q in range(CROSS):
            here = slice(q * GROUP, (q + 1) * GROUP)
            for index, block in ((q, aheads[step]), (CROSS + q, behinds[step])):
                line = jnp.sum(align(block[here]), axis=0, keepdims=True)
                term = vh_ref[index] * line
                vector = term if vector is None else vector + term
        vectors.append(jnp.sum(vector, axis=1, keepdims=True))

    kept = []
    for step in range(steps):
        keep = jnp.concatenate([lane_ref[step]] * (2 * rim), axis=1)
        kept.append(split(outside * keep))
    all_high = jnp.concatenate([piece[0] for piece in kept], axis=0)
    all_low = jnp.concatenate([piece[1] for piece in kept], axis=0)
    removed_all = dot(all_high, out_high, NT) + (dot(all_high, out_low, NT) + dot(all_low, out_high, NT))

    row = iota((basis, LANES), 0)
    lane = iota((basis, LANES), 1)
    systems = []
    for step in range(steps):
        removed = removed_all[step * basis : (step + 1) * basis]
        square = jnp.concatenate(
            [totals[step], jnp.zeros((LANES - basis, LANES), F32)], axis=0
        )
        matrix = (square + square.T)[:basis]
        removed = jnp.concatenate([removed, jnp.zeros((basis, LANES - basis), F32)], axis=1)
        matrix = jnp.where(lane < basis, matrix - removed, 0.0)
        trace = jnp.sum(jnp.where(row == lane, matrix, 0.0), keepdims=True)
        system = jnp.where(row == lane, matrix + RIDGE * trace / basis, matrix)
        systems.append(jnp.where(lane == basis, vectors[step], system))
    top = MARGIN - rim
    low_top = MARGIN + half - 2 * rim
    for step in every:
        window = jnp.where(
            tile == 0,
            template[step, top : top + GROUP, :],
            template[step, low_top : low_top + GROUP, :],
        )
        spread_window[step] = columns_for_bands(window, rim)
    coefficients = solve(systems)
    for step in every:
        reverse = exact(coefficients[step] * vpad_ref[...], hrev_ref[...], TN)
        write_bands(reverse, taps, kernels.at[step])
    founds = []
    copies = []
    for step in every:
        modelled = apply_bands(
            spread_window[step], kernels.at[step], sums.at[step], GROUP, taps, half + rim
        )
        founds.append(target_ref[step] - modelled)
        difference[step, 0] = jnp.where(tile == 0, founds[step][:half], founds[step][rim:])
        copies.append(
            pltpu.make_async_copy(difference.at[step], difference_ref.at[step], sems.at[0, step])
        )
        copies[-1].start()
    for step in every:
        tall = jnp.concatenate(
            [founds[step], jnp.zeros((GROUP - half - rim, columns), F32)], axis=0
        )
        tall = jnp.where(tile == 0, pltpu.roll(tall, rim, 0), tall)
        likelihood[step, 0] = apply_bands(
            columns_for_bands(tall, rim), band_ref, sums.at[step], GROUP, taps, half
        )
        copies.append(
            pltpu.make_async_copy(likelihood.at[step], likelihood_ref.at[step], sems.at[1, step])
        )
        copies[-1].start()
    for copy in copies:
        copy.wait()


def in_vmem(count):
    return [pl.BlockSpec(memory_space=pltpu.VMEM)] * count


def in_smem(count):
    return [pl.BlockSpec(memory_space=pltpu.SMEM)] * count


def run_prepare(tile, vertical, horizontal, psf, own, other, mask, mask_other):
    taps, basis = vertical.shape
    steps, _, half, columns = own.shape
    wide = SHIFTS * GROUP
    shapes = [
        ((wide, wide), BF16), ((wide, wide), BF16),
        ((basis, 3 * TAP_PAD), BF16),
        ((STRIDES, basis, wide), F32),
        ((2 * CROSS, basis, wide), F32),
        ((2 * (taps // 2) * basis, 4 * LANES), BF16), ((2 * (taps // 2) * basis, 4 * LANES), BF16),
        ((basis, LANES), F32), ((basis, LANES), F32),
        ((4 * LANES, (taps + 1) * LANES), BF16),
        ((steps, CROSS * GROUP, columns), BF16), ((steps, CROSS * GROUP, columns), BF16),
        ((steps, wide, columns), BF16), ((steps, wide, columns), BF16),
        ((steps, TAP_PAD, 2 * GROUP), BF16),
        ((steps, 1, LANES), F32),
        ((steps, half + taps // 2, columns), F32),
    ]
    return pl.pallas_call(
        prepare,
        out_shape=[jax.ShapeDtypeStruct(shape, dtype) for shape, dtype in shapes],
        in_specs=in_smem(1) + in_vmem(7),
        out_specs=in_vmem(len(shapes)),
        scratch_shapes=[
            pltpu.VMEM((LANES, LANES), F32),
            pltpu.VMEM((LANES, LANES), F32),
            pltpu.VMEM((TAP_PAD, TAP_PAD), F32),
            pltpu.VMEM((GROUP, columns), F32),
            pltpu.VMEM((TAP_PAD, LANES), F32),
        ],
        compiler_params=pltpu.CompilerParams(vmem_limit_bytes=8 << 20),
        cost_estimate=pl.CostEstimate(flops=4_000_000_000, bytes_accessed=8_000_000, transcendentals=0),
        name="prepare",
    )(tile, vertical, horizontal, psf, own, other, mask, mask_other)


def stage(*refs):
    count = (len(refs) - 1) // 2
    copies = [
        pltpu.make_async_copy(refs[i], refs[count + i], refs[-1].at[i]) for i in range(count)
    ]
    for copy in copies:
        copy.start()
    for copy in copies:
        copy.wait()


def run_stage(*arrays):
    return pl.pallas_call(
        stage,
        out_shape=[jax.ShapeDtypeStruct(array.shape, array.dtype) for array in arrays],
        in_specs=[pl.BlockSpec(memory_space=pl.ANY)] * len(arrays),
        out_specs=in_vmem(len(arrays)),
        scratch_shapes=[pltpu.SemaphoreType.DMA((len(arrays),))],
        compiler_params=pltpu.CompilerParams(vmem_limit_bytes=4 << 20),
        cost_estimate=pl.CostEstimate(flops=0, bytes_accessed=2_000_000, transcendentals=0),
        name="stage",
    )(*arrays)


def run_fit(tile, own, other, prepared, taps):
    steps, _, half, columns = own.shape
    blocks = columns // LANES
    return pl.pallas_call(
        fit,
        out_shape=[jax.ShapeDtypeStruct(own.shape, F32)] * 2,
        in_specs=in_smem(1) + in_vmem(2 + len(prepared)),
        out_specs=[pl.BlockSpec(memory_space=pl.ANY)] * 2,
        scratch_shapes=[
            pltpu.VMEM((steps, GROUP + 2 * MARGIN, columns), F32),
            pltpu.VMEM((steps, GROUP + 2 * MARGIN, LANES), F32),
            pltpu.VMEM((steps, 4 * LANES, (taps + 1) * LANES), BF16),
            pltpu.VMEM((steps, taps, blocks * GROUP, LANES), F32),
            pltpu.VMEM((steps, blocks * GROUP, 4 * LANES), BF16),
            pltpu.VMEM((steps, 1, half, columns), F32),
            pltpu.VMEM((steps, 1, half, columns), F32),
            pltpu.SemaphoreType.DMA((2, steps)),
        ],
        compiler_params=pltpu.CompilerParams(vmem_limit_bytes=20 << 20),
        cost_estimate=pl.CostEstimate(flops=20_000_000_000, bytes_accessed=16_000_000, transcendentals=0),
        name="fit",
    )(tile, own, other, *prepared)


def exchange(block, bit):
    count = lax.axis_size("visit")
    return lax.ppermute(block, "visit", [(i, i ^ bit) for i in range(count)])


def choose(block, arrived, distance, bit):
    count = lax.axis_size("visit")
    holds = jnp.bitwise_and(distance, count - bit) == 0
    return jnp.where(holds.reshape(-1, 1, 1, 1), block, arrived)


def on_device(templates, science, stamp_mask, owner, visit_map, vertical, horizontal, psf):
    swap = [(0, 1), (1, 0)]
    tile = lax.axis_index("tile").astype(jnp.int32).reshape(1)
    count = lax.axis_size("visit")
    arrived = exchange(templates, 1) if count > 1 else templates
    staged = run_stage(templates, science, stamp_mask)
    distance = jnp.bitwise_xor(visit_map[owner], lax.axis_index("visit"))
    arrived, distance, staged = lax.optimization_barrier((arrived, distance, staged))
    block, science, stamp_mask = staged
    block = choose(block, arrived, distance, 1)
    science_other = lax.ppermute(science, "tile", swap)
    mask_other = lax.ppermute(stamp_mask, "tile", swap)
    profiles = run_stage(psf, vertical.T, horizontal.T)
    bit = 2
    prepared = None
    while bit < count:
        arrived = exchange(block, bit)
        bit *= 2
        if bit >= count:
            prepared = run_prepare(
                tile, profiles[1], profiles[2], profiles[0],
                science, science_other, stamp_mask, mask_other,
            )
            arrived, prepared = lax.optimization_barrier((arrived, prepared))
        elif bit == 4:
            arrived, science_other, mask_other, profiles = lax.optimization_barrier(
                (arrived, science_other, mask_other, profiles)
            )
        block = choose(block, arrived, distance, bit // 2)
    block_other = lax.ppermute(block, "tile", swap)
    return tuple(run_fit(tile, block, block_other, prepared, vertical.shape[1]))


def solution(mesh):
    placed = (
        P(None, ("groups", "visit"), "tile", None),
        P(None, ("groups", "visit"), "tile", None),
        P(None, ("groups", "visit"), "tile"),
        P("groups"),
        P("groups"),
        P(),
        P(),
        P(),
    )
    return jax.shard_map(
        on_device,
        mesh=mesh,
        in_specs=placed,
        out_specs=(
            P(None, ("groups", "visit"), "tile", None),
            P(None, ("groups", "visit"), "tile", None),
        ),
        check_vma=False,
    )
```

```python
import jax
import jax.numpy as jnp
from jax import lax
from jax.experimental import pallas as pl
from jax.experimental.pallas import tpu as pltpu
from jax.sharding import PartitionSpec as P

RIDGE = 0.05
F32 = jnp.float32
BF16 = jnp.bfloat16
HIGHEST = lax.Precision.HIGHEST
NN = (((1,), (0,)), ((), ()))
NT = (((1,), (1,)), ((), ()))
TN = (((0,), (0,)), ((), ()))

LANES = 128
GROUP = 64
SHIFTS = 4
STRIDES = 6
CROSS = 3
EDGE_TAPS = 6
TAP_PAD = 32
REST = 32
PANEL = 8
MARGIN = 16
START = 43


def iota(shape, dim):
    return lax.broadcasted_iota(jnp.int32, shape, dim)


def split(x):
    high = x.astype(BF16)
    return high, (x - high.astype(F32)).astype(BF16)


def dot(a, b, dims):
    return lax.dot_general(a, b, dims, preferred_element_type=F32)


def dot3(a, b, dims):
    return dot(a[0], b[0], dims) + (dot(a[0], b[1], dims) + dot(a[1], b[0], dims))


def exact(a, b, dims):
    return lax.dot_general(a, b, dims, precision=HIGHEST, preferred_element_type=F32)


def shift_right(x, amount):
    if amount == 0:
        return x
    return jnp.where(iota(x.shape, 1) >= amount, pltpu.roll(x, amount, 1), 0.0)


def shift_left(x, amount):
    if amount == 0:
        return x
    width = x.shape[1]
    return jnp.where(iota(x.shape, 1) < width - amount, pltpu.roll(x, width - amount, 1), 0.0)


def flip_rows(x):
    count = x.shape[0]
    mirror = (iota((count, count), 0) + iota((count, count), 1) == count - 1).astype(BF16)
    high, low = split(x)
    return dot(mirror, high, NN) + dot(mirror, low, NN)


def store_split(refs, index, x):
    high, low = split(x)
    refs[0][index] = high
    refs[1][index] = low


def write_bands(reverse, taps, ref):
    row = iota((LANES, LANES), 0)
    lane = iota((LANES, LANES), 1)
    ref[3 * LANES + 3 * REST :, :] = jnp.zeros((LANES - 3 * REST, ref.shape[1]), BF16)
    ref[:, taps * LANES :] = jnp.zeros((ref.shape[0], ref.shape[1] - taps * LANES), BF16)
    for tap in range(taps):
        base = jnp.broadcast_to(reverse[tap : tap + 1, :], (LANES, LANES))
        turned = pltpu.roll(base, 0, 1, stride=1, stride_axis=0)
        here = slice(tap * LANES, (tap + 1) * LANES)
        high, low = split(jnp.where(lane <= row, turned, 0.0))
        ref[0:LANES, here] = high
        ref[LANES : 2 * LANES, here] = high
        ref[2 * LANES : 3 * LANES, here] = low
        high, low = split(jnp.where(lane[:REST] > row[:REST], turned[:REST], 0.0))
        ref[3 * LANES : 3 * LANES + REST, here] = high
        ref[3 * LANES + REST : 3 * LANES + 2 * REST, here] = high
        ref[3 * LANES + 2 * REST : 3 * LANES + 3 * REST, here] = low


def prepare(
    tile_ref, vertical_ref, horizontal_ref, psf_ref, own_ref, other_ref, mask_ref, mask_other_ref,
    vb_high, vb_low, vq_ref, hc_ref, vh_ref, edge_high, edge_low, hrev_ref, vpad_ref,
    band_ref, left_high, left_low, right_high, right_low, rows_ref, lane_ref, target_ref,
    v_turned, h_turned, psf_pad, science, chosen,
):
    taps, basis = vertical_ref.shape
    steps = own_ref.shape[0]
    rim = taps // 2
    half = own_ref.shape[2]
    tile = tile_ref[0]
    v_turned[...] = jnp.zeros(v_turned.shape, F32)
    h_turned[...] = jnp.zeros(h_turned.shape, F32)
    psf_pad[...] = jnp.zeros(psf_pad.shape, F32)
    v_turned[:taps, :basis] = vertical_ref[...]
    h_turned[:taps, :basis] = horizontal_ref[...]
    psf_pad[:taps, :taps] = psf_ref[...]
    v_all = v_turned[...].T[:GROUP, :TAP_PAD]
    h_all = h_turned[...].T[:GROUP]
    v = v_all[:basis]
    h = h_all[:basis, :TAP_PAD]
    wide = SHIFTS * GROUP

    def pick(width, index):
        return (iota((TAP_PAD, width), 0) == index).astype(F32)

    lane = (iota((TAP_PAD, wide), 1) + wide - START) % wide
    turn, place = lane // GROUP, lane % GROUP

    def source(shape):
        return (iota(shape, 0) + wide - START - TAP_PAD + 1) % wide

    select = 2 * rim - source((wide, TAP_PAD)) % GROUP == iota((wide, TAP_PAD), 1)
    every = exact(select.astype(F32), jnp.concatenate([v_all] * SHIFTS, axis=0), NT)
    same = source((wide, wide)) // GROUP == iota((wide, wide), 1) // GROUP
    store_split((vb_high, vb_low), (slice(None), slice(None)), jnp.where(same, every, 0.0))

    mirror = iota((TAP_PAD, TAP_PAD), 0) + iota((TAP_PAD, TAP_PAD), 1) == TAP_PAD - 1
    v_high, v_low = split(exact(v, mirror.astype(F32), NN))
    vq_ref[:, 0:TAP_PAD] = v_high
    vq_ref[:, TAP_PAD : 2 * TAP_PAD] = v_high
    vq_ref[:, 2 * TAP_PAD : 3 * TAP_PAD] = v_low

    for q in range(STRIDES):
        pieces = []
        for s in range(SHIFTS):
            distance = SHIFTS * q + s
            pieces.append(pltpu.roll(h_all, (LANES - distance) % LANES, 1))
        both = exact(h_all[:basis], jnp.concatenate(pieces, axis=0), NT)
        if q == 0:
            both = jnp.where(iota(both.shape, 1) < GROUP, 0.5 * both, both)
        hc_ref[q] = both

    down = exact(v, pick(wide, 3 * rim - place), NN)
    up = exact(v, pick(wide, place - rim), NN)
    for q in range(CROSS):
        ahead = exact(h, pick(wide, rim + SHIFTS * q + turn), NN)
        behind = exact(h, pick(wide, rim - SHIFTS * q - turn), NN)
        if q == 0:
            behind = jnp.where(turn[:1] == 0, 0.0, behind)
        vh_ref[q] = down * ahead
        vh_ref[CROSS + q] = up * behind

    narrow = iota((TAP_PAD, LANES), 1)
    part = narrow // (2 * rim)
    column = narrow % (2 * rim)
    used = part < EDGE_TAPS
    spread_v = jnp.concatenate(
        [
            exact(v, pick(LANES, jnp.where(used, EDGE_TAPS * t + part, -1)), NN)
            for t in range(4)
        ],
        axis=1,
    )
    for e in range(rim):
        spread_h = exact(h, pick(LANES, jnp.where(used, column + 2 * rim - e, -1)), NN)
        spread_h += exact(h, pick(LANES, jnp.where(used, column - e - rim, -1)), NN)
        store_split(
            (edge_high, edge_low),
            (slice(e * basis, (e + 1) * basis), slice(None)),
            spread_v * jnp.concatenate([spread_h] * 4, axis=1),
        )

    back = pick(LANES, (LANES - narrow) % LANES)
    hrev_ref[...] = exact(h, back, NN)
    vpad_ref[...] = jnp.zeros(vpad_ref.shape, F32)
    vpad_ref[:, :TAP_PAD] = v
    write_bands(exact(psf_pad[...], back, NN), taps, band_ref)

    for step in range(steps):
        science[pl.ds(half * tile, half), :] = own_ref[step, 0]
        science[pl.ds(half * (1 - tile), half), :] = other_ref[step, 0]
        first = jnp.where(tile == 0, mask_ref[step], mask_other_ref[step]).astype(F32)
        second = jnp.where(tile == 0, mask_other_ref[step], mask_ref[step]).astype(F32)
        mask = jnp.concatenate([first, second], axis=1)
        diagonal = iota((GROUP, GROUP), 0) == iota((GROUP, GROUP), 1)
        column_mask = jnp.sum(jnp.where(diagonal, mask, 0.0), axis=1, keepdims=True)
        masked = science[...] * column_mask
        mirrored = flip_rows(masked)
        for q in range(CROSS):
            store_split(
                (left_high, left_low),
                (step, slice(q * GROUP, (q + 1) * GROUP), slice(None)),
                shift_right(masked, SHIFTS * q),
            )
        for s in range(SHIFTS):
            store_split(
                (right_high, right_low),
                (step, slice(s * GROUP, (s + 1) * GROUP), slice(None)),
                shift_left(mirrored, s),
            )
        chosen[...] = jnp.zeros(chosen.shape, F32)
        single = jnp.concatenate([mask, jnp.zeros((1, GROUP), F32)], axis=1)
        for tap in range(taps):
            place_row = TAP_PAD - 1 - tap
            chosen[place_row : place_row + 1, :] = pltpu.roll(single, (tap - rim) % LANES, 1)
        moved = chosen[...][:, :GROUP]
        rows_ref[step] = jnp.concatenate([moved, moved], axis=1).astype(BF16)
        lane_ref[step] = jnp.concatenate([mask, mask], axis=1).astype(BF16)
        target_ref[step] = jnp.where(
            tile == 0, science[0 : half + rim, :], science[half - rim : 2 * half, :]
        )


def solve(systems):
    count, width = systems[0].shape
    row = iota((count, width), 0)
    lane = iota((count, width), 1)
    for first in range(0, count, PANEL):
        panels = [
            [
                jnp.broadcast_to(system[:, first + j : first + j + 1], (count, width))
                for j in range(PANEL)
            ]
            for system in systems
        ]
        for j in range(PANEL):
            pivot = first + j
            for index, panel in enumerate(panels):
                column = panel[j]
                factor = column * (1.0 / column[pivot : pivot + 1, :])
                factor = jnp.where(row == pivot, 0.0, factor)
                for m in range(j + 1, PANEL):
                    panel[m] = panel[m] - factor * panel[m][pivot : pivot + 1, :]
                system = systems[index]
                systems[index] = system - factor * system[pivot : pivot + 1, :]
    results = []
    for system in systems:
        scale = jnp.sum(jnp.where(row == lane, system, 0.0), axis=1, keepdims=True)
        results.append(system[:, count : count + 1] / scale)
    return results


def columns_for_bands(image, rim):
    rows, columns = image.shape
    padded = pltpu.roll(
        jnp.concatenate([image, jnp.zeros((rows, LANES), F32)], axis=1), rim, 1
    )
    high, low = split(padded)
    lane = iota((rows, LANES), 1)
    blocks = []
    for c in range(columns // LANES):
        here = slice(c * LANES, (c + 1) * LANES)
        there = slice((c + 1) * LANES, (c + 2) * LANES)
        next_high = high[:, there].astype(F32)
        next_low = low[:, there].astype(F32)
        rest = jnp.where(
            lane < REST,
            next_high,
            jnp.where(
                lane < 2 * REST,
                pltpu.roll(next_low, REST, 1),
                jnp.where(lane < 3 * REST, pltpu.roll(next_high, 2 * REST, 1), 0.0),
            ),
        )
        blocks.append(
            jnp.concatenate([high[:, here], low[:, here], high[:, here], rest.astype(BF16)], axis=1)
        )
    return jnp.concatenate(blocks, axis=0)


def apply_bands(left, band_ref, sums, rows, taps, out_rows):
    block_count = left.shape[0] // rows
    for tap in range(0, taps, 2):
        count = min(2, taps - tap)
        both = dot(left, band_ref[:, tap * LANES : (tap + count) * LANES], NN)
        for side in range(count):
            sums[tap + side] = both[:, side * LANES : (side + 1) * LANES]
    blocks = []
    for c in range(block_count):
        total = None
        for tap in range(taps):
            first = c * rows + tap
            term = sums[tap, first : first + out_rows, :]
            total = term if total is None else total + term
        blocks.append(total)
    return jnp.concatenate(blocks, axis=1)


def fit(
    tile_ref, own_ref, other_ref,
    vb_high, vb_low, vq_ref, hc_ref, vh_ref, edge_high, edge_low, hrev_ref, vpad_ref,
    band_ref, left_high, left_low, right_high, right_low, rows_ref, lane_ref, target_ref,
    difference_ref, likelihood_ref,
    template, border, kernels, sums, spread_window, difference, likelihood, sems,
):
    steps = own_ref.shape[0]
    half = own_ref.shape[2]
    columns = own_ref.shape[3]
    basis = hrev_ref.shape[0]
    taps = sums.shape[1]
    rim = taps // 2
    tile = tile_ref[0]
    wide = SHIFTS * GROUP
    place = (iota((GROUP, wide), 1) + wide - START) % wide % GROUP
    other_row = iota((GROUP, wide), 0) + 2 * rim - place
    valid = (other_row >= 0) & (other_row < GROUP) & (place <= 4 * rim)
    every = range(steps)
    border[...] = jnp.zeros(border.shape, F32)
    template[...] = jnp.zeros(template.shape, F32)
    images = []
    for step in every:
        for index, ref in ((tile, own_ref), (1 - tile, other_ref)):
            first = pl.multiple_of(MARGIN + half * index, 16)
            template[step, pl.ds(first, half), :] = ref[step, 0]
        images.append(template[step, MARGIN : MARGIN + GROUP, :])
    mirrored = [flip_rows(image) for image in images]
    lefts = []
    for image in images:
        pieces = [split(shift_right(image, SHIFTS * q)) for q in range(STRIDES)]
        lefts.append([jnp.concatenate([piece[i] for piece in pieces], axis=0) for i in (0, 1)])
    rights = []
    for image in mirrored:
        pieces = [split(shift_left(image, s)) for s in range(SHIFTS)]
        rights.append([jnp.concatenate([piece[i] for piece in pieces], axis=0) for i in (0, 1)])

    stacks = []
    lane = iota((GROUP, LANES), 1)
    at_left = lane % (2 * rim) < rim
    for step, image in enumerate(images):
        far = pltpu.roll(image[:, columns - LANES :], 2 * rim, 1)
        ends = jnp.where(lane < rim, image[:, :LANES], jnp.where(lane < 2 * rim, far, 0.0))
        for g in range(EDGE_TAPS):
            border[step, g, MARGIN : MARGIN + GROUP, :] = (
                pltpu.roll(ends, 2 * rim * g, 1) if g else ends
            )
        chunks = []
        for first in range(0, 4 * EDGE_TAPS, EDGE_TAPS):
            chunk = None
            for g in range(min(EDGE_TAPS, taps - first)):
                line = first + g + MARGIN - rim
                piece = border[step, g, line : line + GROUP, :]
                chunk = piece if chunk is None else chunk + piece
            chunks.append(chunk)
        stacks.append(
            jnp.concatenate([jnp.where(at_left, chunk, 0.0) for chunk in chunks], axis=1)
        )
        stacks.append(
            jnp.concatenate([jnp.where(at_left, 0.0, chunk) for chunk in chunks], axis=1)
        )

    autos = [dot3(lefts[step], rights[step], NT) for step in every]
    aheads = [dot3((left_high[step], left_low[step]), rights[step], NT) for step in every]
    behinds = []
    for step in every:
        near = [piece[: CROSS * GROUP] for piece in lefts[step]]
        behinds.append(dot3(near, (right_high[step], right_low[step]), NT))

    def align(block):
        turned = pltpu.roll(block, 0, 1, stride=1, stride_axis=0)
        return jnp.where(valid, turned, 0.0)

    aligned = []
    for step in every:
        parts = [split(align(autos[step][q * GROUP : (q + 1) * GROUP])) for q in range(STRIDES)]
        aligned.append([jnp.concatenate(part, axis=0) for part in parts])
    products = []
    for step in every:
        gathered = [dot(rows_ref[step], part, NN) for part in aligned[step]]
        turned = [pltpu.roll(part, 0, 1, stride=1, stride_axis=0) for part in gathered]
        products.append(split(jnp.concatenate(turned, axis=0)))
    stack = split(jnp.concatenate(stacks, axis=0))
    outside = dot3((edge_high[...], edge_low[...]), stack, NT)
    partials = [dot3(products[step], (vb_high[...], vb_low[...]), NN) for step in every]
    outer = []
    for step in every:
        here = slice(step * LANES, (step + 1) * LANES)
        outer.append(
            split(
                jnp.concatenate(
                    [outside[e * basis : (e + 1) * basis, here] for e in range(rim)], axis=1
                )
            )
        )
    totals = []
    for step in every:
        total = None
        for q in range(STRIDES):
            high, low = split(partials[step][q * TAP_PAD : (q + 1) * TAP_PAD])
            mixed = dot(vq_ref[...], jnp.concatenate([high, low, high], axis=0), NN)
            term = mixed * hc_ref[q]
            total = term if total is None else total + term
        total = total[:, :LANES] + total[:, LANES:]
        totals.append(total + pltpu.roll(total, GROUP, 1))
    vectors = []
    for step in every:
        vector = None
        for q in range(CROSS):
            here = slice(q * GROUP, (q + 1) * GROUP)
            for index, block in ((q, aheads[step]), (CROSS + q, behinds[step])):
                line = jnp.sum(align(block[here]), axis=0, keepdims=True)
                term = vh_ref[index] * line
                vector = term if vector is None else vector + term
        vectors.append(jnp.sum(vector, axis=1, keepdims=True))

    removals = []
    for step in every:
        high, low = outer[step]
        keep = jnp.concatenate([lane_ref[step]] * rim, axis=1)
        kept_high = high * keep
        first = dot(jnp.concatenate([kept_high.astype(F32), (low * keep).astype(F32)], axis=0).astype(BF16), high, NT)
        removals.append(first[:basis] + (first[basis:] + dot(kept_high, low, NT)))

    row = iota((basis, LANES), 0)
    lane = iota((basis, LANES), 1)
    systems = []
    for step in range(steps):
        removed = removals[step]
        square = jnp.concatenate(
            [totals[step], jnp.zeros((LANES - basis, LANES), F32)], axis=0
        )
        matrix = (square + square.T)[:basis]
        removed = jnp.concatenate([removed, jnp.zeros((basis, LANES - basis), F32)], axis=1)
        matrix = jnp.where(lane < basis, matrix - removed, 0.0)
        trace = jnp.sum(jnp.where(row == lane, matrix, 0.0), keepdims=True)
        system = jnp.where(row == lane, matrix + RIDGE * trace / basis, matrix)
        systems.append(jnp.where(lane == basis, vectors[step], system))
    top = MARGIN - rim
    low_top = MARGIN + half - 2 * rim
    for step in every:
        window = jnp.where(
            tile == 0,
            template[step, top : top + GROUP, :],
            template[step, low_top : low_top + GROUP, :],
        )
        spread_window[step] = columns_for_bands(window, rim)
    coefficients = solve(systems)
    for step in every:
        reverse = exact(coefficients[step] * vpad_ref[...], hrev_ref[...], TN)
        write_bands(reverse, taps, kernels.at[step])
    founds = []
    copies = []
    for step in every:
        modelled = apply_bands(
            spread_window[step], kernels.at[step], sums.at[step], GROUP, taps, half + rim
        )
        founds.append(target_ref[step] - modelled)
        difference[step, 0] = jnp.where(tile == 0, founds[step][:half], founds[step][rim:])
        copies.append(
            pltpu.make_async_copy(difference.at[step], difference_ref.at[step], sems.at[0, step])
        )
        copies[-1].start()
    for step in every:
        tall = jnp.concatenate(
            [founds[step], jnp.zeros((GROUP - half - rim, columns), F32)], axis=0
        )
        tall = jnp.where(tile == 0, pltpu.roll(tall, rim, 0), tall)
        likelihood[step, 0] = apply_bands(
            columns_for_bands(tall, rim), band_ref, sums.at[step], GROUP, taps, half
        )
        copies.append(
            pltpu.make_async_copy(likelihood.at[step], likelihood_ref.at[step], sems.at[1, step])
        )
        copies[-1].start()
    for copy in copies:
        copy.wait()


def in_vmem(count):
    return [pl.BlockSpec(memory_space=pltpu.VMEM)] * count


def in_smem(count):
    return [pl.BlockSpec(memory_space=pltpu.SMEM)] * count


def run_prepare(tile, vertical, horizontal, psf, own, other, mask, mask_other):
    taps, basis = vertical.shape
    steps, _, half, columns = own.shape
    wide = SHIFTS * GROUP
    shapes = [
        ((wide, wide), BF16), ((wide, wide), BF16),
        ((basis, 3 * TAP_PAD), BF16),
        ((STRIDES, basis, wide), F32),
        ((2 * CROSS, basis, wide), F32),
        ((taps // 2 * basis, 4 * LANES), BF16), ((taps // 2 * basis, 4 * LANES), BF16),
        ((basis, LANES), F32), ((basis, LANES), F32),
        ((4 * LANES, (taps + 1) * LANES), BF16),
        ((steps, CROSS * GROUP, columns), BF16), ((steps, CROSS * GROUP, columns), BF16),
        ((steps, wide, columns), BF16), ((steps, wide, columns), BF16),
        ((steps, TAP_PAD, 2 * GROUP), BF16),
        ((steps, 1, LANES), BF16),
        ((steps, half + taps // 2, columns), F32),
    ]
    return pl.pallas_call(
        prepare,
        out_shape=[jax.ShapeDtypeStruct(shape, dtype) for shape, dtype in shapes],
        in_specs=in_smem(1) + in_vmem(7),
        out_specs=in_vmem(len(shapes)),
        scratch_shapes=[
            pltpu.VMEM((LANES, LANES), F32),
            pltpu.VMEM((LANES, LANES), F32),
            pltpu.VMEM((TAP_PAD, TAP_PAD), F32),
            pltpu.VMEM((GROUP, columns), F32),
            pltpu.VMEM((TAP_PAD, LANES), F32),
        ],
        compiler_params=pltpu.CompilerParams(vmem_limit_bytes=8 << 20),
        cost_estimate=pl.CostEstimate(flops=4_000_000_000, bytes_accessed=8_000_000, transcendentals=0),
        name="prepare",
    )(tile, vertical, horizontal, psf, own, other, mask, mask_other)


def stage(*refs):
    count = (len(refs) - 1) // 2
    copies = [
        pltpu.make_async_copy(refs[i], refs[count + i], refs[-1].at[i]) for i in range(count)
    ]
    for copy in copies:
        copy.start()
    for copy in copies:
        copy.wait()


def run_stage(*arrays):
    return pl.pallas_call(
        stage,
        out_shape=[jax.ShapeDtypeStruct(array.shape, array.dtype) for array in arrays],
        in_specs=[pl.BlockSpec(memory_space=pl.ANY)] * len(arrays),
        out_specs=in_vmem(len(arrays)),
        scratch_shapes=[pltpu.SemaphoreType.DMA((len(arrays),))],
        compiler_params=pltpu.CompilerParams(vmem_limit_bytes=4 << 20),
        cost_estimate=pl.CostEstimate(flops=0, bytes_accessed=2_000_000, transcendentals=0),
        name="stage",
    )(*arrays)


def run_fit(tile, own, other, prepared, taps):
    steps, _, half, columns = own.shape
    blocks = columns // LANES
    return pl.pallas_call(
        fit,
        out_shape=[jax.ShapeDtypeStruct(own.shape, F32)] * 2,
        in_specs=in_smem(1) + in_vmem(2 + len(prepared)),
        out_specs=[pl.BlockSpec(memory_space=pl.ANY)] * 2,
        scratch_shapes=[
            pltpu.VMEM((steps, GROUP + 2 * MARGIN, columns), F32),
            pltpu.VMEM((steps, EDGE_TAPS, GROUP + 2 * MARGIN, LANES), F32),
            pltpu.VMEM((steps, 4 * LANES, (taps + 1) * LANES), BF16),
            pltpu.VMEM((steps, taps, blocks * GROUP, LANES), F32),
            pltpu.VMEM((steps, blocks * GROUP, 4 * LANES), BF16),
            pltpu.VMEM((steps, 1, half, columns), F32),
            pltpu.VMEM((steps, 1, half, columns), F32),
            pltpu.SemaphoreType.DMA((2, steps)),
        ],
        compiler_params=pltpu.CompilerParams(vmem_limit_bytes=20 << 20),
        cost_estimate=pl.CostEstimate(flops=20_000_000_000, bytes_accessed=16_000_000, transcendentals=0),
        name="fit",
    )(tile, own, other, *prepared)


def exchange(block, bit):
    count = lax.axis_size("visit")
    return lax.ppermute(block, "visit", [(i, i ^ bit) for i in range(count)])


def choose(block, arrived, distance, bit):
    count = lax.axis_size("visit")
    holds = jnp.bitwise_and(distance, count - bit) == 0
    return jnp.where(holds.reshape(-1, 1, 1, 1), block, arrived)


def on_device(templates, science, stamp_mask, owner, visit_map, vertical, horizontal, psf):
    swap = [(0, 1), (1, 0)]
    tile = lax.axis_index("tile").astype(jnp.int32).reshape(1)
    count = lax.axis_size("visit")
    arrived = exchange(templates, 1) if count > 1 else templates
    staged = run_stage(templates, science, stamp_mask)
    distance = jnp.bitwise_xor(visit_map[owner], lax.axis_index("visit"))
    arrived, distance, staged = lax.optimization_barrier((arrived, distance, staged))
    block, science, stamp_mask = staged
    block = choose(block, arrived, distance, 1)
    science_other = lax.ppermute(science, "tile", swap)
    mask_other = lax.ppermute(stamp_mask, "tile", swap)
    profiles = run_stage(psf, vertical.T, horizontal.T)
    bit = 2
    prepared = None
    while bit < count:
        arrived = exchange(block, bit)
        bit *= 2
        if bit >= count:
            prepared = run_prepare(
                tile, profiles[1], profiles[2], profiles[0],
                science, science_other, stamp_mask, mask_other,
            )
            arrived, prepared = lax.optimization_barrier((arrived, prepared))
        elif bit == 4:
            arrived, science_other, mask_other, profiles = lax.optimization_barrier(
                (arrived, science_other, mask_other, profiles)
            )
        block = choose(block, arrived, distance, bit // 2)
    block_other = lax.ppermute(block, "tile", swap)
    return tuple(run_fit(tile, block, block_other, prepared, vertical.shape[1]))


def solution(mesh):
    placed = (
        P(None, ("groups", "visit"), "tile", None),
        P(None, ("groups", "visit"), "tile", None),
        P(None, ("groups", "visit"), "tile"),
        P("groups"),
        P("groups"),
        P(),
        P(),
        P(),
    )
    return jax.shard_map(
        on_device,
        mesh=mesh,
        in_specs=placed,
        out_specs=(
            P(None, ("groups", "visit"), "tile", None),
            P(None, ("groups", "visit"), "tile", None),
        ),
        check_vma=False,
    )
```

```python
import jax
import jax.numpy as jnp
from jax import lax
from jax.experimental import pallas as pl
from jax.experimental.pallas import tpu as pltpu
from jax.sharding import PartitionSpec as P

RIDGE = 0.05
F32 = jnp.float32
BF16 = jnp.bfloat16
HIGHEST = lax.Precision.HIGHEST
NN = (((1,), (0,)), ((), ()))
NT = (((1,), (1,)), ((), ()))
TN = (((0,), (0,)), ((), ()))

LANES = 128
GROUP = 64
SHIFTS = 4
STRIDES = 6
CROSS = 3
EDGE_TAPS = 6
TAP_PAD = 32
REST = 32
PANEL = 8
MARGIN = 16
START = 43


def iota(shape, dim):
    return lax.broadcasted_iota(jnp.int32, shape, dim)


def split(x):
    high = x.astype(BF16)
    return high, (x - high.astype(F32)).astype(BF16)


def dot(a, b, dims):
    return lax.dot_general(a, b, dims, preferred_element_type=F32)


def dot3(a, b, dims):
    return dot(a[0], b[0], dims) + (dot(a[0], b[1], dims) + dot(a[1], b[0], dims))


def exact(a, b, dims):
    return lax.dot_general(a, b, dims, precision=HIGHEST, preferred_element_type=F32)


def shift_right(x, amount):
    if amount == 0:
        return x
    return jnp.where(iota(x.shape, 1) >= amount, pltpu.roll(x, amount, 1), 0.0)


def shift_left(x, amount):
    if amount == 0:
        return x
    width = x.shape[1]
    return jnp.where(iota(x.shape, 1) < width - amount, pltpu.roll(x, width - amount, 1), 0.0)


def flip_rows(x):
    count = x.shape[0]
    mirror = (iota((count, count), 0) + iota((count, count), 1) == count - 1).astype(BF16)
    high, low = split(x)
    return dot(mirror, high, NN) + dot(mirror, low, NN)


def store_split(refs, index, x):
    high, low = split(x)
    refs[0][index] = high
    refs[1][index] = low


def write_bands(reverse, taps, ref):
    row = iota((LANES, LANES), 0)
    lane = iota((LANES, LANES), 1)
    ref[3 * LANES + 3 * REST :, :] = jnp.zeros((LANES - 3 * REST, ref.shape[1]), BF16)
    ref[:, taps * LANES :] = jnp.zeros((ref.shape[0], ref.shape[1] - taps * LANES), BF16)
    for tap in range(taps):
        base = jnp.broadcast_to(reverse[tap : tap + 1, :], (LANES, LANES))
        turned = pltpu.roll(base, 0, 1, stride=1, stride_axis=0)
        here = slice(tap * LANES, (tap + 1) * LANES)
        high, low = split(jnp.where(lane <= row, turned, 0.0))
        ref[0:LANES, here] = high
        ref[LANES : 2 * LANES, here] = high
        ref[2 * LANES : 3 * LANES, here] = low
        high, low = split(jnp.where(lane[:REST] > row[:REST], turned[:REST], 0.0))
        ref[3 * LANES : 3 * LANES + REST, here] = high
        ref[3 * LANES + REST : 3 * LANES + 2 * REST, here] = high
        ref[3 * LANES + 2 * REST : 3 * LANES + 3 * REST, here] = low


def prepare(
    tile_ref, vertical_ref, horizontal_ref, psf_ref, own_ref, other_ref, mask_ref, mask_other_ref,
    vb_high, vb_low, vq_ref, hc_ref, vh_ref, edge_high, edge_low, hrev_ref, vpad_ref,
    band_ref, left_high, left_low, right_high, right_low, rows_ref, lane_ref, target_ref,
    v_turned, h_turned, psf_pad, science, chosen,
):
    taps, basis = vertical_ref.shape
    steps = own_ref.shape[0]
    rim = taps // 2
    half = own_ref.shape[2]
    tile = tile_ref[0]
    v_turned[...] = jnp.zeros(v_turned.shape, F32)
    h_turned[...] = jnp.zeros(h_turned.shape, F32)
    psf_pad[...] = jnp.zeros(psf_pad.shape, F32)
    v_turned[:taps, :basis] = vertical_ref[...]
    h_turned[:taps, :basis] = horizontal_ref[...]
    psf_pad[:taps, :taps] = psf_ref[...]
    v_all = v_turned[...].T[:GROUP, :TAP_PAD]
    h_all = h_turned[...].T[:GROUP]
    v = v_all[:basis]
    h = h_all[:basis, :TAP_PAD]
    wide = SHIFTS * GROUP

    def pick(width, index):
        return (iota((TAP_PAD, width), 0) == index).astype(F32)

    lane = (iota((TAP_PAD, wide), 1) + wide - START) % wide
    turn, place = lane // GROUP, lane % GROUP

    def source(shape):
        return (iota(shape, 0) + wide - START - TAP_PAD + 1) % wide

    select = 2 * rim - source((wide, TAP_PAD)) % GROUP == iota((wide, TAP_PAD), 1)
    every = exact(select.astype(F32), jnp.concatenate([v_all] * SHIFTS, axis=0), NT)
    same = source((wide, wide)) // GROUP == iota((wide, wide), 1) // GROUP
    store_split((vb_high, vb_low), (slice(None), slice(None)), jnp.where(same, every, 0.0))

    mirror = iota((TAP_PAD, TAP_PAD), 0) + iota((TAP_PAD, TAP_PAD), 1) == TAP_PAD - 1
    v_high, v_low = split(exact(v, mirror.astype(F32), NN))
    vq_ref[:, 0:TAP_PAD] = v_high
    vq_ref[:, TAP_PAD : 2 * TAP_PAD] = v_high
    vq_ref[:, 2 * TAP_PAD : 3 * TAP_PAD] = v_low

    for q in range(STRIDES):
        pieces = []
        for s in range(SHIFTS):
            distance = SHIFTS * q + s
            pieces.append(pltpu.roll(h_all, (LANES - distance) % LANES, 1))
        both = exact(h_all[:basis], jnp.concatenate(pieces, axis=0), NT)
        if q == 0:
            both = jnp.where(iota(both.shape, 1) < GROUP, 0.5 * both, both)
        hc_ref[q] = both

    down = exact(v, pick(wide, 3 * rim - place), NN)
    up = exact(v, pick(wide, place - rim), NN)
    for q in range(CROSS):
        ahead = exact(h, pick(wide, rim + SHIFTS * q + turn), NN)
        behind = exact(h, pick(wide, rim - SHIFTS * q - turn), NN)
        if q == 0:
            behind = jnp.where(turn[:1] == 0, 0.0, behind)
        vh_ref[q] = down * ahead
        vh_ref[CROSS + q] = up * behind

    narrow = iota((TAP_PAD, LANES), 1)
    part = narrow // (2 * rim)
    column = narrow % (2 * rim)
    used = part < EDGE_TAPS
    spread_v = jnp.concatenate(
        [
            exact(v, pick(LANES, jnp.where(used, EDGE_TAPS * t + part, -1)), NN)
            for t in range(4)
        ],
        axis=1,
    )
    for e in range(rim):
        spread_h = exact(h, pick(LANES, jnp.where(used, column + 2 * rim - e, -1)), NN)
        spread_h += exact(h, pick(LANES, jnp.where(used, column - e - rim, -1)), NN)
        store_split(
            (edge_high, edge_low),
            (slice(e * basis, (e + 1) * basis), slice(None)),
            spread_v * jnp.concatenate([spread_h] * 4, axis=1),
        )

    back = pick(LANES, (LANES - narrow) % LANES)
    hrev_ref[...] = exact(h, back, NN)
    vpad_ref[...] = jnp.zeros(vpad_ref.shape, F32)
    vpad_ref[:, :TAP_PAD] = v
    write_bands(exact(psf_pad[...], back, NN), taps, band_ref)

    for step in range(steps):
        science[pl.ds(half * tile, half), :] = own_ref[step, 0]
        science[pl.ds(half * (1 - tile), half), :] = other_ref[step, 0]
        first = jnp.where(tile == 0, mask_ref[step], mask_other_ref[step]).astype(F32)
        second = jnp.where(tile == 0, mask_other_ref[step], mask_ref[step]).astype(F32)
        mask = jnp.concatenate([first, second], axis=1)
        diagonal = iota((GROUP, GROUP), 0) == iota((GROUP, GROUP), 1)
        column_mask = jnp.sum(jnp.where(diagonal, mask, 0.0), axis=1, keepdims=True)
        masked = science[...] * column_mask
        mirrored = flip_rows(masked)
        for q in range(CROSS):
            store_split(
                (left_high, left_low),
                (step, slice(q * GROUP, (q + 1) * GROUP), slice(None)),
                shift_right(masked, SHIFTS * q),
            )
        for s in range(SHIFTS):
            store_split(
                (right_high, right_low),
                (step, slice(s * GROUP, (s + 1) * GROUP), slice(None)),
                shift_left(mirrored, s),
            )
        chosen[...] = jnp.zeros(chosen.shape, F32)
        single = jnp.concatenate([mask, jnp.zeros((1, GROUP), F32)], axis=1)
        for tap in range(taps):
            place_row = TAP_PAD - 1 - tap
            chosen[place_row : place_row + 1, :] = pltpu.roll(single, (tap - rim) % LANES, 1)
        moved = chosen[...][:, :GROUP]
        rows_ref[step] = jnp.concatenate([moved, moved], axis=1).astype(BF16)
        lane_ref[step] = jnp.concatenate([mask, mask], axis=1).astype(BF16)
        target_ref[step] = jnp.where(
            tile == 0, science[0 : half + rim, :], science[half - rim : 2 * half, :]
        )


def solve(systems):
    count, width = systems[0].shape
    row = iota((count, width), 0)
    lane = iota((count, width), 1)
    for first in range(0, count, PANEL):
        panels = [
            [
                jnp.broadcast_to(system[:, first + j : first + j + 1], (count, width))
                for j in range(PANEL)
            ]
            for system in systems
        ]
        for j in range(PANEL):
            pivot = first + j
            for index, panel in enumerate(panels):
                column = panel[j]
                factor = column * (1.0 / column[pivot : pivot + 1, :])
                factor = jnp.where(row == pivot, 0.0, factor)
                for m in range(j + 1, PANEL):
                    panel[m] = panel[m] - factor * panel[m][pivot : pivot + 1, :]
                system = systems[index]
                systems[index] = system - factor * system[pivot : pivot + 1, :]
    results = []
    for system in systems:
        scale = jnp.sum(jnp.where(row == lane, system, 0.0), axis=1, keepdims=True)
        results.append(system[:, count : count + 1] / scale)
    return results


def columns_for_bands(image, rim):
    rows, columns = image.shape
    padded = pltpu.roll(
        jnp.concatenate([image, jnp.zeros((rows, LANES), F32)], axis=1), rim, 1
    )
    high, low = split(padded)
    lane = iota((rows, LANES), 1)
    blocks = []
    for c in range(columns // LANES):
        here = slice(c * LANES, (c + 1) * LANES)
        there = slice((c + 1) * LANES, (c + 2) * LANES)
        next_high = high[:, there].astype(F32)
        next_low = low[:, there].astype(F32)
        rest = jnp.where(
            lane < REST,
            next_high,
            jnp.where(
                lane < 2 * REST,
                pltpu.roll(next_low, REST, 1),
                jnp.where(lane < 3 * REST, pltpu.roll(next_high, 2 * REST, 1), 0.0),
            ),
        )
        blocks.append(
            jnp.concatenate([high[:, here], low[:, here], high[:, here], rest.astype(BF16)], axis=1)
        )
    return jnp.concatenate(blocks, axis=0)


def apply_bands(left, band_ref, sums, rows, taps, out_rows):
    block_count = left.shape[0] // rows
    for tap in range(0, taps, 2):
        count = min(2, taps - tap)
        both = dot(left, band_ref[:, tap * LANES : (tap + count) * LANES], NN)
        for side in range(count):
            sums[tap + side] = both[:, side * LANES : (side + 1) * LANES]
    blocks = []
    for c in range(block_count):
        total = None
        for tap in range(taps):
            first = c * rows + tap
            term = sums[tap, first : first + out_rows, :]
            total = term if total is None else total + term
        blocks.append(total)
    return jnp.concatenate(blocks, axis=1)


def fit(
    tile_ref, own_ref, other_ref,
    vb_high, vb_low, vq_ref, hc_ref, vh_ref, edge_high, edge_low, hrev_ref, vpad_ref,
    band_ref, left_high, left_low, right_high, right_low, rows_ref, lane_ref, target_ref,
    difference_ref, likelihood_ref,
    template, border, kernels, sums, spread_window, difference, likelihood, sems,
):
    steps = own_ref.shape[0]
    half = own_ref.shape[2]
    columns = own_ref.shape[3]
    basis = hrev_ref.shape[0]
    taps = sums.shape[1]
    rim = taps // 2
    tile = tile_ref[0]
    wide = SHIFTS * GROUP
    place = (iota((GROUP, wide), 1) + wide - START) % wide % GROUP
    other_row = iota((GROUP, wide), 0) + 2 * rim - place
    valid = (other_row >= 0) & (other_row < GROUP) & (place <= 4 * rim)
    every = range(steps)
    border[...] = jnp.zeros(border.shape, F32)
    template[...] = jnp.zeros(template.shape, F32)
    images = []
    for step in every:
        for index, ref in ((tile, own_ref), (1 - tile, other_ref)):
            first = pl.multiple_of(MARGIN + half * index, 16)
            template[step, pl.ds(first, half), :] = ref[step, 0]
        images.append(template[step, MARGIN : MARGIN + GROUP, :])
    mirrored = [flip_rows(image) for image in images]
    lefts = []
    for image in images:
        pieces = [split(shift_right(image, SHIFTS * q)) for q in range(STRIDES)]
        lefts.append([jnp.concatenate([piece[i] for piece in pieces], axis=0) for i in (0, 1)])
    rights = []
    for image in mirrored:
        pieces = [split(shift_left(image, s)) for s in range(SHIFTS)]
        rights.append([jnp.concatenate([piece[i] for piece in pieces], axis=0) for i in (0, 1)])

    stacks = []
    lane = iota((GROUP, LANES), 1)
    at_left = lane % (2 * rim) < rim
    for step, image in enumerate(images):
        far = pltpu.roll(image[:, columns - LANES :], 2 * rim, 1)
        ends = jnp.where(lane < rim, image[:, :LANES], jnp.where(lane < 2 * rim, far, 0.0))
        for g in range(EDGE_TAPS):
            border[step, g, MARGIN : MARGIN + GROUP, :] = (
                pltpu.roll(ends, 2 * rim * g, 1) if g else ends
            )
        chunks = []
        for first in range(0, 4 * EDGE_TAPS, EDGE_TAPS):
            chunk = None
            for g in range(min(EDGE_TAPS, taps - first)):
                line = first + g + MARGIN - rim
                piece = border[step, g, line : line + GROUP, :]
                chunk = piece if chunk is None else chunk + piece
            chunks.append(chunk)
        stacks.append(
            jnp.concatenate([jnp.where(at_left, chunk, 0.0) for chunk in chunks], axis=1)
        )
        stacks.append(
            jnp.concatenate([jnp.where(at_left, 0.0, chunk) for chunk in chunks], axis=1)
        )

    autos = [dot3(lefts[step], rights[step], NT) for step in every]
    aheads = [dot3((left_high[step], left_low[step]), rights[step], NT) for step in every]
    behinds = []
    for step in every:
        near = [piece[: CROSS * GROUP] for piece in lefts[step]]
        behinds.append(dot3(near, (right_high[step], right_low[step]), NT))

    def align(block):
        turned = pltpu.roll(block, 0, 1, stride=1, stride_axis=0)
        return jnp.where(valid, turned, 0.0)

    aligned = []
    for step in every:
        parts = [split(align(autos[step][q * GROUP : (q + 1) * GROUP])) for q in range(STRIDES)]
        aligned.append([jnp.concatenate(part, axis=0) for part in parts])
    products = []
    for step in every:
        gathered = [dot(rows_ref[step], part, NN) for part in aligned[step]]
        turned = [pltpu.roll(part, 0, 1, stride=1, stride_axis=0) for part in gathered]
        products.append(split(jnp.concatenate(turned, axis=0)))
    stack = split(jnp.concatenate(stacks, axis=0))
    outside = dot3((edge_high[...], edge_low[...]), stack, NT)
    partials = [dot3(products[step], (vb_high[...], vb_low[...]), NN) for step in every]
    outer = []
    for step in every:
        here = slice(step * LANES, (step + 1) * LANES)
        outer.append(
            split(
                jnp.concatenate(
                    [outside[e * basis : (e + 1) * basis, here] for e in range(rim)], axis=1
                )
            )
        )
    totals = []
    for step in every:
        total = None
        for q in range(STRIDES):
            high, low = split(partials[step][q * TAP_PAD : (q + 1) * TAP_PAD])
            mixed = dot(vq_ref[...], jnp.concatenate([high, low, high], axis=0), NN)
            term = mixed * hc_ref[q]
            total = term if total is None else total + term
        total = total[:, :LANES] + total[:, LANES:]
        totals.append(total + pltpu.roll(total, GROUP, 1))
    vectors = []
    for step in every:
        vector = None
        for q in range(CROSS):
            here = slice(q * GROUP, (q + 1) * GROUP)
            for index, block in ((q, aheads[step]), (CROSS + q, behinds[step])):
                line = jnp.sum(align(block[here]), axis=0, keepdims=True)
                term = vh_ref[index] * line
                vector = term if vector is None else vector + term
        vectors.append(jnp.sum(vector, axis=1, keepdims=True))

    removals = []
    for step in every:
        high, low = outer[step]
        keep = jnp.concatenate([lane_ref[step]] * rim, axis=1)
        kept_high = high * keep
        first = dot(jnp.concatenate([kept_high.astype(F32), (low * keep).astype(F32)], axis=0).astype(BF16), high, NT)
        removals.append(first[:basis] + (first[basis:] + dot(kept_high, low, NT)))

    row = iota((basis, LANES), 0)
    lane = iota((basis, LANES), 1)
    systems = []
    for step in range(steps):
        removed = removals[step]
        square = jnp.concatenate(
            [totals[step], jnp.zeros((LANES - basis, LANES), F32)], axis=0
        )
        matrix = (square + square.T)[:basis]
        removed = jnp.concatenate([removed, jnp.zeros((basis, LANES - basis), F32)], axis=1)
        matrix = jnp.where(lane < basis, matrix - removed, 0.0)
        trace = jnp.sum(jnp.where(row == lane, matrix, 0.0), keepdims=True)
        system = jnp.where(row == lane, matrix + RIDGE * trace / basis, matrix)
        systems.append(jnp.where(lane == basis, vectors[step], system))
    top = MARGIN - rim
    low_top = MARGIN + half - 2 * rim
    for step in every:
        window = jnp.where(
            tile == 0,
            template[step, top : top + GROUP, :],
            template[step, low_top : low_top + GROUP, :],
        )
        spread_window[step] = columns_for_bands(window, rim)
    coefficients = solve(systems)
    for step in every:
        reverse = exact(coefficients[step] * vpad_ref[...], hrev_ref[...], TN)
        write_bands(reverse, taps, kernels.at[step])
    founds = []
    copies = []
    for step in every:
        modelled = apply_bands(
            spread_window[step], kernels.at[step], sums.at[step], GROUP, taps, half + rim
        )
        founds.append(target_ref[step] - modelled)
        difference[step, 0] = jnp.where(tile == 0, founds[step][:half], founds[step][rim:])
        copies.append(
            pltpu.make_async_copy(difference.at[step], difference_ref.at[step], sems.at[0, step])
        )
        copies[-1].start()
    for step in every:
        tall = jnp.concatenate(
            [founds[step], jnp.zeros((GROUP - half - rim, columns), F32)], axis=0
        )
        tall = jnp.where(tile == 0, pltpu.roll(tall, rim, 0), tall)
        likelihood[step, 0] = apply_bands(
            columns_for_bands(tall, rim), band_ref, sums.at[step], GROUP, taps, half
        )
        copies.append(
            pltpu.make_async_copy(likelihood.at[step], likelihood_ref.at[step], sems.at[1, step])
        )
        copies[-1].start()
    for copy in copies:
        copy.wait()


def in_vmem(count):
    return [pl.BlockSpec(memory_space=pltpu.VMEM)] * count


def in_smem(count):
    return [pl.BlockSpec(memory_space=pltpu.SMEM)] * count


def run_prepare(tile, vertical, horizontal, psf, own, other, mask, mask_other):
    taps, basis = vertical.shape
    steps, _, half, columns = own.shape
    wide = SHIFTS * GROUP
    shapes = [
        ((wide, wide), BF16), ((wide, wide), BF16),
        ((basis, 3 * TAP_PAD), BF16),
        ((STRIDES, basis, wide), F32),
        ((2 * CROSS, basis, wide), F32),
        ((taps // 2 * basis, 4 * LANES), BF16), ((taps // 2 * basis, 4 * LANES), BF16),
        ((basis, LANES), F32), ((basis, LANES), F32),
        ((4 * LANES, (taps + 1) * LANES), BF16),
        ((steps, CROSS * GROUP, columns), BF16), ((steps, CROSS * GROUP, columns), BF16),
        ((steps, wide, columns), BF16), ((steps, wide, columns), BF16),
        ((steps, TAP_PAD, 2 * GROUP), BF16),
        ((steps, 1, LANES), BF16),
        ((steps, half + taps // 2, columns), F32),
    ]
    return pl.pallas_call(
        prepare,
        out_shape=[jax.ShapeDtypeStruct(shape, dtype) for shape, dtype in shapes],
        in_specs=in_smem(1) + in_vmem(7),
        out_specs=in_vmem(len(shapes)),
        scratch_shapes=[
            pltpu.VMEM((LANES, LANES), F32),
            pltpu.VMEM((LANES, LANES), F32),
            pltpu.VMEM((TAP_PAD, TAP_PAD), F32),
            pltpu.VMEM((GROUP, columns), F32),
            pltpu.VMEM((TAP_PAD, LANES), F32),
        ],
        compiler_params=pltpu.CompilerParams(vmem_limit_bytes=8 << 20),
        cost_estimate=pl.CostEstimate(flops=4_000_000_000, bytes_accessed=8_000_000, transcendentals=0),
        name="prepare",
    )(tile, vertical, horizontal, psf, own, other, mask, mask_other)


def stage(*refs):
    count = (len(refs) - 1) // 2
    copies = [
        pltpu.make_async_copy(refs[i], refs[count + i], refs[-1].at[i]) for i in range(count)
    ]
    for copy in copies:
        copy.start()
    for copy in copies:
        copy.wait()


def run_stage(*arrays):
    return pl.pallas_call(
        stage,
        out_shape=[jax.ShapeDtypeStruct(array.shape, array.dtype) for array in arrays],
        in_specs=[pl.BlockSpec(memory_space=pl.ANY)] * len(arrays),
        out_specs=in_vmem(len(arrays)),
        scratch_shapes=[pltpu.SemaphoreType.DMA((len(arrays),))],
        compiler_params=pltpu.CompilerParams(vmem_limit_bytes=4 << 20),
        cost_estimate=pl.CostEstimate(flops=0, bytes_accessed=2_000_000, transcendentals=0),
        name="stage",
    )(*arrays)


def run_fit(tile, own, other, prepared, taps):
    steps, _, half, columns = own.shape
    blocks = columns // LANES
    return pl.pallas_call(
        fit,
        out_shape=[jax.ShapeDtypeStruct(own.shape, F32)] * 2,
        in_specs=in_smem(1) + in_vmem(2 + len(prepared)),
        out_specs=[pl.BlockSpec(memory_space=pl.ANY)] * 2,
        scratch_shapes=[
            pltpu.VMEM((steps, GROUP + 2 * MARGIN, columns), F32),
            pltpu.VMEM((steps, EDGE_TAPS, GROUP + 2 * MARGIN, LANES), F32),
            pltpu.VMEM((steps, 4 * LANES, (taps + 1) * LANES), BF16),
            pltpu.VMEM((steps, taps, blocks * GROUP, LANES), F32),
            pltpu.VMEM((steps, blocks * GROUP, 4 * LANES), BF16),
            pltpu.VMEM((steps, 1, half, columns), F32),
            pltpu.VMEM((steps, 1, half, columns), F32),
            pltpu.SemaphoreType.DMA((2, steps)),
        ],
        compiler_params=pltpu.CompilerParams(vmem_limit_bytes=20 << 20),
        cost_estimate=pl.CostEstimate(flops=20_000_000_000, bytes_accessed=16_000_000, transcendentals=0),
        name="fit",
    )(tile, own, other, *prepared)


def exchange(block, bit):
    count = lax.axis_size("visit")
    return lax.ppermute(block, "visit", [(i, i ^ bit) for i in range(count)])


def choose(block, arrived, distance, unseen):
    holds = jnp.bitwise_and(distance, unseen) == 0
    return jnp.where(holds.reshape(-1, 1, 1, 1), block, arrived)


def on_device(templates, science, stamp_mask, owner, visit_map, vertical, horizontal, psf):
    swap = [(0, 1), (1, 0)]
    tile = lax.axis_index("tile").astype(jnp.int32).reshape(1)
    count = lax.axis_size("visit")
    bits = [1 << place for place in reversed(range((count - 1).bit_length()))]
    unseen = count - 1
    block = templates
    prepared = None
    for turn, bit in enumerate(bits):
        arrived = exchange(block, bit)
        if turn == 0:
            staged = run_stage(
                templates, science, stamp_mask, psf, vertical.T, horizontal.T
            )
            distance = jnp.bitwise_xor(visit_map[owner], lax.axis_index("visit"))
            arrived, distance, staged = lax.optimization_barrier((arrived, distance, staged))
            block, science, stamp_mask, psf, vertical_t, horizontal_t = staged
            science_other = lax.ppermute(science, "tile", swap)
            mask_other = lax.ppermute(stamp_mask, "tile", swap)
        if turn == 1:
            prepared = run_prepare(
                tile, vertical_t, horizontal_t, psf,
                science, science_other, stamp_mask, mask_other,
            )
            arrived, prepared = lax.optimization_barrier((arrived, prepared))
        block = choose(block, arrived, distance, unseen)
        unseen -= bit
    block_other = lax.ppermute(block, "tile", swap)
    return tuple(run_fit(tile, block, block_other, prepared, vertical.shape[1]))


def solution(mesh):
    placed = (
        P(None, ("groups", "visit"), "tile", None),
        P(None, ("groups", "visit"), "tile", None),
        P(None, ("groups", "visit"), "tile"),
        P("groups"),
        P("groups"),
        P(),
        P(),
        P(),
    )
    return jax.shard_map(
        on_device,
        mesh=mesh,
        in_specs=placed,
        out_specs=(
            P(None, ("groups", "visit"), "tile", None),
            P(None, ("groups", "visit"), "tile", None),
        ),
        check_vma=False,
    )
```

```python
import jax
import jax.numpy as jnp
from jax import lax
from jax.experimental import pallas as pl
from jax.experimental.pallas import tpu as pltpu
from jax.sharding import PartitionSpec as P

RIDGE = 0.05
F32 = jnp.float32
BF16 = jnp.bfloat16
HIGHEST = lax.Precision.HIGHEST
NN = (((1,), (0,)), ((), ()))
NT = (((1,), (1,)), ((), ()))
TN = (((0,), (0,)), ((), ()))

LANES = 128
GROUP = 64
SHIFTS = 4
STRIDES = 6
CROSS = 3
EDGE_TAPS = 6
TAP_PAD = 32
REST = 32
PANEL = 8
MARGIN = 16
START = 43


def iota(shape, dim):
    return lax.broadcasted_iota(jnp.int32, shape, dim)


def split(x):
    high = x.astype(BF16)
    return high, (x - high.astype(F32)).astype(BF16)


def dot(a, b, dims):
    return lax.dot_general(a, b, dims, preferred_element_type=F32)


def dot3(a, b, dims):
    return dot(a[0], b[0], dims) + (dot(a[0], b[1], dims) + dot(a[1], b[0], dims))


def exact(a, b, dims):
    return lax.dot_general(a, b, dims, precision=HIGHEST, preferred_element_type=F32)


def shift_right(x, amount):
    if amount == 0:
        return x
    return jnp.where(iota(x.shape, 1) >= amount, pltpu.roll(x, amount, 1), 0.0)


def shift_left(x, amount):
    if amount == 0:
        return x
    width = x.shape[1]
    return jnp.where(iota(x.shape, 1) < width - amount, pltpu.roll(x, width - amount, 1), 0.0)


def flip_rows(x):
    count = x.shape[0]
    mirror = (iota((count, count), 0) + iota((count, count), 1) == count - 1).astype(BF16)
    high, low = split(x)
    return dot(mirror, high, NN) + dot(mirror, low, NN)


def store_split(refs, index, x):
    high, low = split(x)
    refs[0][index] = high
    refs[1][index] = low


def write_bands(reverse, taps, ref):
    row = iota((LANES, LANES), 0)
    lane = iota((LANES, LANES), 1)
    ref[3 * LANES + 3 * REST :, :] = jnp.zeros((LANES - 3 * REST, ref.shape[1]), BF16)
    ref[:, taps * LANES :] = jnp.zeros((ref.shape[0], ref.shape[1] - taps * LANES), BF16)
    for tap in range(taps):
        base = jnp.broadcast_to(reverse[tap : tap + 1, :], (LANES, LANES))
        turned = pltpu.roll(base, 0, 1, stride=1, stride_axis=0)
        here = slice(tap * LANES, (tap + 1) * LANES)
        high, low = split(jnp.where(lane <= row, turned, 0.0))
        ref[0:LANES, here] = high
        ref[LANES : 2 * LANES, here] = high
        ref[2 * LANES : 3 * LANES, here] = low
        high, low = split(jnp.where(lane[:REST] > row[:REST], turned[:REST], 0.0))
        ref[3 * LANES : 3 * LANES + REST, here] = high
        ref[3 * LANES + REST : 3 * LANES + 2 * REST, here] = high
        ref[3 * LANES + 2 * REST : 3 * LANES + 3 * REST, here] = low


def prepare(
    tile_ref, vertical_ref, horizontal_ref, psf_ref, own_ref, other_ref, mask_ref, mask_other_ref,
    vb_high, vb_low, vq_ref, hc_ref, vh_ref, edge_high, edge_low, hrev_ref, vpad_ref,
    band_ref, left_high, left_low, right_high, right_low, rows_ref, lane_ref, target_ref,
    v_turned, h_turned, psf_pad, science, chosen,
):
    taps, basis = vertical_ref.shape
    steps = own_ref.shape[0]
    rim = taps // 2
    half = own_ref.shape[2]
    tile = tile_ref[0]
    v_turned[...] = jnp.zeros(v_turned.shape, F32)
    h_turned[...] = jnp.zeros(h_turned.shape, F32)
    psf_pad[...] = jnp.zeros(psf_pad.shape, F32)
    v_turned[:taps, :basis] = vertical_ref[...]
    h_turned[:taps, :basis] = horizontal_ref[...]
    psf_pad[:taps, :taps] = psf_ref[...]
    v_all = v_turned[...].T[:GROUP, :TAP_PAD]
    h_all = h_turned[...].T[:GROUP]
    v = v_all[:basis]
    h = h_all[:basis, :TAP_PAD]
    wide = SHIFTS * GROUP

    def pick(width, index):
        return (iota((TAP_PAD, width), 0) == index).astype(F32)

    lane = (iota((TAP_PAD, wide), 1) + wide - START) % wide
    turn, place = lane // GROUP, lane % GROUP

    def source(shape):
        return (iota(shape, 0) + wide - START - TAP_PAD + 1) % wide

    select = 2 * rim - source((wide, TAP_PAD)) % GROUP == iota((wide, TAP_PAD), 1)
    every = exact(select.astype(F32), jnp.concatenate([v_all] * SHIFTS, axis=0), NT)
    same = source((wide, wide)) // GROUP == iota((wide, wide), 1) // GROUP
    store_split((vb_high, vb_low), (slice(None), slice(None)), jnp.where(same, every, 0.0))

    mirror = iota((TAP_PAD, TAP_PAD), 0) + iota((TAP_PAD, TAP_PAD), 1) == TAP_PAD - 1
    v_high, v_low = split(exact(v, mirror.astype(F32), NN))
    vq_ref[:, 0:TAP_PAD] = v_high
    vq_ref[:, TAP_PAD : 2 * TAP_PAD] = v_high
    vq_ref[:, 2 * TAP_PAD : 3 * TAP_PAD] = v_low

    for q in range(STRIDES):
        pieces = []
        for s in range(SHIFTS):
            distance = SHIFTS * q + s
            pieces.append(pltpu.roll(h_all, (LANES - distance) % LANES, 1))
        both = exact(h_all[:basis], jnp.concatenate(pieces, axis=0), NT)
        if q == 0:
            both = jnp.where(iota(both.shape, 1) < GROUP, 0.5 * both, both)
        hc_ref[q] = both

    down = exact(v, pick(wide, 3 * rim - place), NN)
    up = exact(v, pick(wide, place - rim), NN)
    for q in range(CROSS):
        ahead = exact(h, pick(wide, rim + SHIFTS * q + turn), NN)
        behind = exact(h, pick(wide, rim - SHIFTS * q - turn), NN)
        if q == 0:
            behind = jnp.where(turn[:1] == 0, 0.0, behind)
        vh_ref[q] = down * ahead
        vh_ref[CROSS + q] = up * behind

    narrow = iota((TAP_PAD, LANES), 1)
    part = narrow // (2 * rim)
    column = narrow % (2 * rim)
    used = part < EDGE_TAPS
    spread_v = jnp.concatenate(
        [
            exact(v, pick(LANES, jnp.where(used, EDGE_TAPS * t + part, -1)), NN)
            for t in range(4)
        ],
        axis=1,
    )
    for e in range(rim):
        spread_h = exact(h, pick(LANES, jnp.where(used, column + 2 * rim - e, -1)), NN)
        spread_h += exact(h, pick(LANES, jnp.where(used, column - e - rim, -1)), NN)
        store_split(
            (edge_high, edge_low),
            (slice(e * basis, (e + 1) * basis), slice(None)),
            spread_v * jnp.concatenate([spread_h] * 4, axis=1),
        )

    back = pick(LANES, (LANES - narrow) % LANES)
    hrev_ref[...] = exact(h, back, NN)
    vpad_ref[...] = jnp.zeros(vpad_ref.shape, F32)
    vpad_ref[:, :TAP_PAD] = v
    write_bands(exact(psf_pad[...], back, NN), taps, band_ref)

    for step in range(steps):
        science[pl.ds(half * tile, half), :] = own_ref[step, 0]
        science[pl.ds(half * (1 - tile), half), :] = other_ref[step, 0]
        first = jnp.where(tile == 0, mask_ref[step], mask_other_ref[step]).astype(F32)
        second = jnp.where(tile == 0, mask_other_ref[step], mask_ref[step]).astype(F32)
        mask = jnp.concatenate([first, second], axis=1)
        diagonal = iota((GROUP, GROUP), 0) == iota((GROUP, GROUP), 1)
        column_mask = jnp.sum(jnp.where(diagonal, mask, 0.0), axis=1, keepdims=True)
        masked = science[...] * column_mask
        mirrored = flip_rows(masked)
        for q in range(CROSS):
            store_split(
                (left_high, left_low),
                (step, slice(q * GROUP, (q + 1) * GROUP), slice(None)),
                shift_right(masked, SHIFTS * q),
            )
        for s in range(SHIFTS):
            store_split(
                (right_high, right_low),
                (step, slice(s * GROUP, (s + 1) * GROUP), slice(None)),
                shift_left(mirrored, s),
            )
        chosen[...] = jnp.zeros(chosen.shape, F32)
        single = jnp.concatenate([mask, jnp.zeros((1, GROUP), F32)], axis=1)
        for tap in range(taps):
            place_row = TAP_PAD - 1 - tap
            chosen[place_row : place_row + 1, :] = pltpu.roll(single, (tap - rim) % LANES, 1)
        moved = chosen[...][:, :GROUP]
        rows_ref[step] = jnp.concatenate([moved, moved], axis=1).astype(BF16)
        lane_ref[step] = jnp.concatenate([mask, mask], axis=1).astype(BF16)
        target_ref[step] = jnp.where(
            tile == 0, science[0 : half + rim, :], science[half - rim : 2 * half, :]
        )


def solve(systems):
    count, width = systems[0].shape
    row = iota((count, width), 0)
    lane = iota((count, width), 1)
    for first in range(0, count, PANEL):
        panels = [
            [
                jnp.broadcast_to(system[:, first + j : first + j + 1], (count, width))
                for j in range(PANEL)
            ]
            for system in systems
        ]
        for j in range(PANEL):
            pivot = first + j
            for index, panel in enumerate(panels):
                column = panel[j]
                factor = column * (1.0 / column[pivot : pivot + 1, :])
                factor = jnp.where(row == pivot, 0.0, factor)
                for m in range(j + 1, PANEL):
                    panel[m] = panel[m] - factor * panel[m][pivot : pivot + 1, :]
                system = systems[index]
                systems[index] = system - factor * system[pivot : pivot + 1, :]
    results = []
    for system in systems:
        scale = jnp.sum(jnp.where(row == lane, system, 0.0), axis=1, keepdims=True)
        results.append(system[:, count : count + 1] / scale)
    return results


def columns_for_bands(image, rim):
    rows, columns = image.shape
    padded = pltpu.roll(
        jnp.concatenate([image, jnp.zeros((rows, LANES), F32)], axis=1), rim, 1
    )
    high, low = split(padded)
    lane = iota((rows, LANES), 1)
    blocks = []
    for c in range(columns // LANES):
        here = slice(c * LANES, (c + 1) * LANES)
        there = slice((c + 1) * LANES, (c + 2) * LANES)
        next_high = high[:, there].astype(F32)
        next_low = low[:, there].astype(F32)
        rest = jnp.where(
            lane < REST,
            next_high,
            jnp.where(
                lane < 2 * REST,
                pltpu.roll(next_low, REST, 1),
                jnp.where(lane < 3 * REST, pltpu.roll(next_high, 2 * REST, 1), 0.0),
            ),
        )
        blocks.append(
            jnp.concatenate([high[:, here], low[:, here], high[:, here], rest.astype(BF16)], axis=1)
        )
    return jnp.concatenate(blocks, axis=0)


def apply_bands(left, band_ref, sums, rows, taps, out_rows):
    block_count = left.shape[0] // rows
    for tap in range(0, taps, 2):
        count = min(2, taps - tap)
        both = dot(left, band_ref[:, tap * LANES : (tap + count) * LANES], NN)
        for side in range(count):
            sums[tap + side] = both[:, side * LANES : (side + 1) * LANES]
    blocks = []
    for c in range(block_count):
        total = None
        for tap in range(taps):
            first = c * rows + tap
            term = sums[tap, first : first + out_rows, :]
            total = term if total is None else total + term
        blocks.append(total)
    return jnp.concatenate(blocks, axis=1)


def fit(
    tile_ref, own_ref, other_ref,
    vb_high, vb_low, vq_ref, hc_ref, vh_ref, edge_high, edge_low, hrev_ref, vpad_ref,
    band_ref, left_high, left_low, right_high, right_low, rows_ref, lane_ref, target_ref,
    difference_ref, likelihood_ref,
    template, border, kernels, sums, spread_window, difference, likelihood, sems,
):
    steps = own_ref.shape[0]
    half = own_ref.shape[2]
    columns = own_ref.shape[3]
    basis = hrev_ref.shape[0]
    taps = sums.shape[1]
    rim = taps // 2
    tile = tile_ref[0]
    wide = SHIFTS * GROUP
    place = (iota((GROUP, wide), 1) + wide - START) % wide % GROUP
    other_row = iota((GROUP, wide), 0) + 2 * rim - place
    valid = (other_row >= 0) & (other_row < GROUP) & (place <= 4 * rim)
    every = range(steps)
    border[...] = jnp.zeros(border.shape, F32)
    template[...] = jnp.zeros(template.shape, F32)
    images = []
    for step in every:
        for index, ref in ((tile, own_ref), (1 - tile, other_ref)):
            first = pl.multiple_of(MARGIN + half * index, 16)
            template[step, pl.ds(first, half), :] = ref[step, 0]
        images.append(template[step, MARGIN : MARGIN + GROUP, :])
    mirrored = [flip_rows(image) for image in images]
    lefts = []
    for image in images:
        pieces = [split(shift_right(image, SHIFTS * q)) for q in range(STRIDES)]
        lefts.append([jnp.concatenate([piece[i] for piece in pieces], axis=0) for i in (0, 1)])
    rights = []
    for image in mirrored:
        pieces = [split(shift_left(image, s)) for s in range(SHIFTS)]
        rights.append([jnp.concatenate([piece[i] for piece in pieces], axis=0) for i in (0, 1)])

    stacks = []
    lane = iota((GROUP, LANES), 1)
    at_left = lane % (2 * rim) < rim
    for step, image in enumerate(images):
        far = pltpu.roll(image[:, columns - LANES :], 2 * rim, 1)
        ends = jnp.where(lane < rim, image[:, :LANES], jnp.where(lane < 2 * rim, far, 0.0))
        for g in range(EDGE_TAPS):
            border[step, g, MARGIN : MARGIN + GROUP, :] = (
                pltpu.roll(ends, 2 * rim * g, 1) if g else ends
            )
        chunks = []
        for first in range(0, 4 * EDGE_TAPS, EDGE_TAPS):
            chunk = None
            for g in range(min(EDGE_TAPS, taps - first)):
                line = first + g + MARGIN - rim
                piece = border[step, g, line : line + GROUP, :]
                chunk = piece if chunk is None else chunk + piece
            chunks.append(chunk)
        stacks.append(
            jnp.concatenate([jnp.where(at_left, chunk, 0.0) for chunk in chunks], axis=1)
        )
        stacks.append(
            jnp.concatenate([jnp.where(at_left, 0.0, chunk) for chunk in chunks], axis=1)
        )

    autos = [dot3(lefts[step], rights[step], NT) for step in every]
    aheads = [dot3((left_high[step], left_low[step]), rights[step], NT) for step in every]
    behinds = []
    for step in every:
        near = [piece[: CROSS * GROUP] for piece in lefts[step]]
        behinds.append(dot3(near, (right_high[step], right_low[step]), NT))

    def align(block):
        turned = pltpu.roll(block, 0, 1, stride=1, stride_axis=0)
        return jnp.where(valid, turned, 0.0)

    aligned = []
    for step in every:
        parts = [split(align(autos[step][q * GROUP : (q + 1) * GROUP])) for q in range(STRIDES)]
        aligned.append([jnp.concatenate(part, axis=0) for part in parts])
    products = []
    for step in every:
        gathered = [dot(rows_ref[step], part, NN) for part in aligned[step]]
        turned = [pltpu.roll(part, 0, 1, stride=1, stride_axis=0) for part in gathered]
        products.append(split(jnp.concatenate(turned, axis=0)))
    stack = split(jnp.concatenate(stacks, axis=0))
    outside = dot3((edge_high[...], edge_low[...]), stack, NT)
    partials = [dot3(products[step], (vb_high[...], vb_low[...]), NN) for step in every]
    outer = []
    for step in every:
        here = slice(step * LANES, (step + 1) * LANES)
        outer.append(
            split(
                jnp.concatenate(
                    [outside[e * basis : (e + 1) * basis, here] for e in range(rim)], axis=1
                )
            )
        )
    totals = []
    for step in every:
        total = None
        for q in range(STRIDES):
            high, low = split(partials[step][q * TAP_PAD : (q + 1) * TAP_PAD])
            mixed = dot(vq_ref[...], jnp.concatenate([high, low, high], axis=0), NN)
            term = mixed * hc_ref[q]
            total = term if total is None else total + term
        total = total[:, :LANES] + total[:, LANES:]
        totals.append(total + pltpu.roll(total, GROUP, 1))
    vectors = []
    for step in every:
        vector = None
        for q in range(CROSS):
            here = slice(q * GROUP, (q + 1) * GROUP)
            for index, block in ((q, aheads[step]), (CROSS + q, behinds[step])):
                line = jnp.sum(align(block[here]), axis=0, keepdims=True)
                term = vh_ref[index] * line
                vector = term if vector is None else vector + term
        vectors.append(jnp.sum(vector, axis=1, keepdims=True))

    removals = []
    for step in every:
        high, low = outer[step]
        keep = jnp.concatenate([lane_ref[step]] * rim, axis=1)
        kept_high = high * keep
        first = dot(jnp.concatenate([kept_high.astype(F32), (low * keep).astype(F32)], axis=0).astype(BF16), high, NT)
        removals.append(first[:basis] + (first[basis:] + dot(kept_high, low, NT)))

    row = iota((basis, LANES), 0)
    lane = iota((basis, LANES), 1)
    systems = []
    for step in range(steps):
        removed = removals[step]
        square = jnp.concatenate(
            [totals[step], jnp.zeros((LANES - basis, LANES), F32)], axis=0
        )
        matrix = (square + square.T)[:basis]
        removed = jnp.concatenate([removed, jnp.zeros((basis, LANES - basis), F32)], axis=1)
        matrix = jnp.where(lane < basis, matrix - removed, 0.0)
        trace = jnp.sum(jnp.where(row == lane, matrix, 0.0), keepdims=True)
        system = jnp.where(row == lane, matrix + RIDGE * trace / basis, matrix)
        systems.append(jnp.where(lane == basis, vectors[step], system))
    top = MARGIN - rim
    low_top = MARGIN + half - 2 * rim
    for step in every:
        window = jnp.where(
            tile == 0,
            template[step, top : top + GROUP, :],
            template[step, low_top : low_top + GROUP, :],
        )
        spread_window[step] = columns_for_bands(window, rim)
    coefficients = solve(systems)
    for step in every:
        reverse = exact(coefficients[step] * vpad_ref[...], hrev_ref[...], TN)
        write_bands(reverse, taps, kernels.at[step])
    founds = []
    copies = []
    for step in every:
        modelled = apply_bands(
            spread_window[step], kernels.at[step], sums.at[step], GROUP, taps, half + rim
        )
        founds.append(target_ref[step] - modelled)
        difference[step, 0] = jnp.where(tile == 0, founds[step][:half], founds[step][rim:])
        copies.append(
            pltpu.make_async_copy(difference.at[step], difference_ref.at[step], sems.at[0, step])
        )
        copies[-1].start()
    for step in every:
        tall = jnp.concatenate(
            [founds[step], jnp.zeros((GROUP - half - rim, columns), F32)], axis=0
        )
        tall = jnp.where(tile == 0, pltpu.roll(tall, rim, 0), tall)
        likelihood[step, 0] = apply_bands(
            columns_for_bands(tall, rim), band_ref, sums.at[step], GROUP, taps, half
        )
        copies.append(
            pltpu.make_async_copy(likelihood.at[step], likelihood_ref.at[step], sems.at[1, step])
        )
        copies[-1].start()
    for copy in copies:
        copy.wait()


def in_vmem(count):
    return [pl.BlockSpec(memory_space=pltpu.VMEM)] * count


def in_smem(count):
    return [pl.BlockSpec(memory_space=pltpu.SMEM)] * count


def run_prepare(tile, vertical, horizontal, psf, own, other, mask, mask_other):
    taps, basis = vertical.shape
    steps, _, half, columns = own.shape
    wide = SHIFTS * GROUP
    shapes = [
        ((wide, wide), BF16), ((wide, wide), BF16),
        ((basis, 3 * TAP_PAD), BF16),
        ((STRIDES, basis, wide), F32),
        ((2 * CROSS, basis, wide), F32),
        ((taps // 2 * basis, 4 * LANES), BF16), ((taps // 2 * basis, 4 * LANES), BF16),
        ((basis, LANES), F32), ((basis, LANES), F32),
        ((4 * LANES, (taps + 1) * LANES), BF16),
        ((steps, CROSS * GROUP, columns), BF16), ((steps, CROSS * GROUP, columns), BF16),
        ((steps, wide, columns), BF16), ((steps, wide, columns), BF16),
        ((steps, TAP_PAD, 2 * GROUP), BF16),
        ((steps, 1, LANES), BF16),
        ((steps, half + taps // 2, columns), F32),
    ]
    return pl.pallas_call(
        prepare,
        out_shape=[jax.ShapeDtypeStruct(shape, dtype) for shape, dtype in shapes],
        in_specs=in_smem(1) + in_vmem(7),
        out_specs=in_vmem(len(shapes)),
        scratch_shapes=[
            pltpu.VMEM((LANES, LANES), F32),
            pltpu.VMEM((LANES, LANES), F32),
            pltpu.VMEM((TAP_PAD, TAP_PAD), F32),
            pltpu.VMEM((GROUP, columns), F32),
            pltpu.VMEM((TAP_PAD, LANES), F32),
        ],
        compiler_params=pltpu.CompilerParams(vmem_limit_bytes=8 << 20),
        cost_estimate=pl.CostEstimate(flops=4_000_000_000, bytes_accessed=8_000_000, transcendentals=0),
        name="prepare",
    )(tile, vertical, horizontal, psf, own, other, mask, mask_other)


def stage(*refs):
    count = (len(refs) - 1) // 2
    copies = [
        pltpu.make_async_copy(refs[i], refs[count + i], refs[-1].at[i]) for i in range(count)
    ]
    for copy in copies:
        copy.start()
    for copy in copies:
        copy.wait()


def run_stage(*arrays):
    return pl.pallas_call(
        stage,
        out_shape=[jax.ShapeDtypeStruct(array.shape, array.dtype) for array in arrays],
        in_specs=[pl.BlockSpec(memory_space=pl.ANY)] * len(arrays),
        out_specs=in_vmem(len(arrays)),
        scratch_shapes=[pltpu.SemaphoreType.DMA((len(arrays),))],
        compiler_params=pltpu.CompilerParams(vmem_limit_bytes=4 << 20),
        cost_estimate=pl.CostEstimate(flops=0, bytes_accessed=2_000_000, transcendentals=0),
        name="stage",
    )(*arrays)


def run_fit(tile, own, other, prepared, taps):
    steps, _, half, columns = own.shape
    blocks = columns // LANES
    return pl.pallas_call(
        fit,
        out_shape=[jax.ShapeDtypeStruct(own.shape, F32)] * 2,
        in_specs=in_smem(1) + in_vmem(2 + len(prepared)),
        out_specs=[pl.BlockSpec(memory_space=pl.ANY)] * 2,
        scratch_shapes=[
            pltpu.VMEM((steps, GROUP + 2 * MARGIN, columns), F32),
            pltpu.VMEM((steps, EDGE_TAPS, GROUP + 2 * MARGIN, LANES), F32),
            pltpu.VMEM((steps, 4 * LANES, (taps + 1) * LANES), BF16),
            pltpu.VMEM((steps, taps, blocks * GROUP, LANES), F32),
            pltpu.VMEM((steps, blocks * GROUP, 4 * LANES), BF16),
            pltpu.VMEM((steps, 1, half, columns), F32),
            pltpu.VMEM((steps, 1, half, columns), F32),
            pltpu.SemaphoreType.DMA((2, steps)),
        ],
        compiler_params=pltpu.CompilerParams(vmem_limit_bytes=20 << 20),
        cost_estimate=pl.CostEstimate(flops=20_000_000_000, bytes_accessed=16_000_000, transcendentals=0),
        name="fit",
    )(tile, own, other, *prepared)


def exchange(block, bit):
    count = lax.axis_size("visit")
    return lax.ppermute(block, "visit", [(i, i ^ bit) for i in range(count)])


def choose(block, arrived, distance, unseen):
    holds = jnp.bitwise_and(distance, unseen) == 0
    return jnp.where(holds.reshape(-1, 1, 1, 1), block, arrived)


def on_device(templates, science, stamp_mask, owner, visit_map, vertical, horizontal, psf):
    swap = [(0, 1), (1, 0)]
    tile = lax.axis_index("tile").astype(jnp.int32).reshape(1)
    count = lax.axis_size("visit")
    bits = [1 << place for place in reversed(range((count - 1).bit_length()))]
    unseen = count - 1
    block = templates
    prepared = None
    for turn, bit in enumerate(bits):
        arrived = exchange(block, bit)
        if turn == 0:
            staged = run_stage(templates, science, stamp_mask)
            distance = jnp.bitwise_xor(visit_map[owner], lax.axis_index("visit"))
            arrived, distance, staged = lax.optimization_barrier((arrived, distance, staged))
            block, science, stamp_mask = staged
        if turn == 1:
            science_other = lax.ppermute(science, "tile", swap)
            mask_other = lax.ppermute(stamp_mask, "tile", swap)
            profiles = run_stage(psf, vertical.T, horizontal.T)
            arrived, science_other, mask_other, profiles = lax.optimization_barrier(
                (arrived, science_other, mask_other, profiles)
            )
        if turn == len(bits) - 1:
            prepared = run_prepare(
                tile, profiles[1], profiles[2], profiles[0],
                science, science_other, stamp_mask, mask_other,
            )
            arrived, prepared = lax.optimization_barrier((arrived, prepared))
        block = choose(block, arrived, distance, unseen)
        unseen -= bit
    block_other = lax.ppermute(block, "tile", swap)
    return tuple(run_fit(tile, block, block_other, prepared, vertical.shape[1]))


def solution(mesh):
    placed = (
        P(None, ("groups", "visit"), "tile", None),
        P(None, ("groups", "visit"), "tile", None),
        P(None, ("groups", "visit"), "tile"),
        P("groups"),
        P("groups"),
        P(),
        P(),
        P(),
    )
    return jax.shard_map(
        on_device,
        mesh=mesh,
        in_specs=placed,
        out_specs=(
            P(None, ("groups", "visit"), "tile", None),
            P(None, ("groups", "visit"), "tile", None),
        ),
        check_vma=False,
    )
```
